128 devices in a mesh: kv: 4 (over y), seq: 32 (over z, x, core).
Axes of the slice: x: 4, y: 4, z: 4, core: 2. Of those that a mesh axis runs over, the one named last changes fastest.
Arguments:
- page_cache: bfloat16 [2048, 2, 8, 128, 128], P('seq', None, 'kv'), may hold values from -9 to 64
- keep_list: int32 [2048, 128], P('seq'), may hold values from 0 to 1, as said below
- fold_weight: float32 [2048, 128], P('seq'), may hold values from 0.1 to 10
- page_table: int32 [256, 8], replicated, may hold values from 0 to 2047, as said below
- lengths: int32 [256], replicated, may hold values from 1 to 1024, 163840 in all
- queries: bfloat16 [256, 16, 128], P('seq', 'kv'), may hold values from -6 to 40
- fresh_entries: bfloat16 [256, 2, 8, 128], P('seq', None, 'kv'), may hold values from -6 to 6
- out_weight: bfloat16 [2048, 2048], P('kv'), may hold values from -0.125 to 0.125
Outputs:
- packed_cache: bfloat16 [2048, 2, 8, 128, 128], P('seq', None, 'kv')
- packed_mass: bfloat16 [2048, 128], P('seq')
- attended: bfloat16 [256, 2048], P('seq', 'kv')
- projected: bfloat16 [256, 2048], P('seq', 'kv')
The draws below stay inside these ranges and needn't reach their ends.
Inputs may be any that keep to these rules, and one draw needn't show every extreme that they name: `page_table`: every physical page appears exactly once. Of the 64 pages of the requests held by one index of seq, exactly 2 lie on each index of seq. `keep_list`: every page keeps at least one and drops at least one of its 128 slots.
All inputs are finite; a program needn't handle non-finite values.
Results may differ from the reference program's by a relative error of at most 0.015.
Values may be sent and summed in bfloat16 or wider, within the bound.
A program may use at most 128 MiB of HBM per device.

```python
import math
import jax
import jax.numpy as jnp
import numpy as np
from jax import lax

D = 2048
HQ = 16
KVH = 8
HD = 128
PSZ = 128
MAXP = 8
PD = 64
PAGES = 2048
REQS = 256


def draw_page_table(key, part):
    seq_count = PAGES // PD
    peer_pages = PD // seq_count
    base = jnp.repeat(jnp.arange(seq_count, dtype=jnp.int32), peer_pages)
    source_keys = jax.random.split(jax.random.fold_in(key, 11), seq_count)
    holder = jax.vmap(lambda one: jax.random.permutation(one, base))(source_keys)
    earlier = jnp.arange(PD)[None, :] < jnp.arange(PD)[:, None]
    same = holder[:, :, None] == holder[:, None, :]
    within = jnp.sum(jnp.logical_and(same, earlier[None]), axis=2).astype(jnp.int32)
    order_rank = jnp.arange(seq_count, dtype=jnp.int32)[:, None] * peer_pages + within
    slot_keys = jax.random.split(jax.random.fold_in(key, 12), seq_count)
    slot_perm = jax.vmap(lambda one: jax.random.permutation(one, PD))(slot_keys).astype(jnp.int32)
    slot = slot_perm[holder, order_rank]
    physical = holder * PD + slot
    return physical.reshape(REQS, MAXP).astype(jnp.int32)


def draw_keep_list(key, part):
    first, second, third, fourth = jax.random.split(jax.random.fold_in(key, 21), 4)
    level = jax.random.randint(first, (PAGES, 1), 16, 112)
    ticket = jax.random.randint(second, (PAGES, PSZ), 0, 128)
    keep_mask = ticket < level
    forced_keep = jax.random.randint(third, (PAGES, 1), 0, PSZ)
    offset = jax.random.randint(fourth, (PAGES, 1), 1, PSZ)
    forced_drop = (forced_keep + offset) % PSZ
    slot_index = jnp.arange(PSZ)[None, :]
    keep_mask = jnp.where(slot_index == forced_keep, True, keep_mask)
    keep_mask = jnp.where(slot_index == forced_drop, False, keep_mask)
    return keep_mask.astype(jnp.int32)


def draw_queries(key, part):
    shape = (REQS, HQ, HD)
    values = jnp.clip(jax.random.normal(jax.random.fold_in(key, 32), shape, jnp.float32), -6.0, 6.0)
    return values.astype(jnp.bfloat16)


def draw_page_cache(key, part):
    shape = (PAGES, 2, KVH, PSZ, HD)
    key_mask = (jnp.arange(2) == 0).reshape(1, 2, 1, 1, 1)
    noise = jnp.clip(jax.random.normal(jax.random.fold_in(key, 42), shape, jnp.float32), -6.0, 6.0)
    values = noise * jnp.where(key_mask, 1.5, 1.0)
    return values.astype(jnp.bfloat16)


def steps_of(own_key, dims, pieces, least, largest):
    gain = 1.0
    for dim, shards_of in pieces:
        heights = jax.random.uniform(jax.random.fold_in(jax.random.fold_in(own_key, 6), dim), (shards_of,), jnp.float32, least / len(pieces), largest / len(pieces))
        gain = gain * jnp.repeat(jnp.exp(heights), dims[dim] // shards_of).reshape((-1,) + (1,) * (len(dims) - 1 - dim))
    return gain


def profile(count, total, most, lean):
    loads = [(1 << 20) // math.isqrt(standing ** lean) + 1 for standing in range(2, count + 1)]
    spare, counts = total - most - (count - 1), [1] * (count - 1)
    while spare > 0:
        movable = [i for i in range(count - 1) if counts[i] < most]
        whole, remaining = sum([loads[i] for i in movable]), spare
        for i in movable:
            addition = min(most - counts[i], max(1, remaining * loads[i] // whole), spare)
            counts[i] = counts[i] + addition
            spare = spare - addition
    return np.array([most] + counts)


def uneven(rng, number_of, total, bound, slope):
    if number_of == 2:
        one = jax.random.randint(rng, (), max(1, total - bound), min(bound, total - 1) + 1)
        return jnp.stack([one, total - one])
    sizes = jnp.asarray(profile(number_of, total, bound, slope), jnp.int32)
    couples = (number_of - 1) // 2
    giver, taker = sizes[1:1 + 2 * couples:2], sizes[2:2 + 2 * couples:2]
    room = jnp.minimum(giver - 1, bound - taker)
    moved = jax.random.randint(jax.random.fold_in(rng, 1), (couples,), 0, 1 << 20) % (room + 1)
    sizes = sizes.at[1:1 + 2 * couples:2].set(giver - moved).at[2:2 + 2 * couples:2].set(taker + moved)
    return sizes[jax.random.permutation(jax.random.fold_in(rng, 2), number_of)]


def gaussian(key, extent, spread, most, pieces=(), kind=jnp.bfloat16):
    entries = jax.random.normal(key, extent, jnp.float32) * spread
    if len(pieces) > 0:
        entries = steps_of(key, extent, pieces, -0.22, 0.18) * entries
    return jnp.clip(entries, min=-most, max=most).astype(kind)


def setup_inputs(seed: int = 0) -> dict:
    splits = jax.random.split(jax.random.key(seed), 9)
    page_cache = draw_page_cache(jax.random.fold_in(splits[8], 71), 0)
    keep_list = draw_keep_list(jax.random.fold_in(splits[8], 71), 0)
    fold_weight = jnp.clip(jnp.exp(math.log(10.0) - 4.6051702 * jax.random.uniform(splits[2], (PAGES, PSZ), jnp.float32) ** steps_of(splits[2], (PAGES, PSZ), ((0, 32),), -0.2, 0.2)), 0.1, 10.0)
    page_table = draw_page_table(jax.random.fold_in(splits[8], 71), 0)
    lengths = uneven(splits[4], REQS, REQS * MAXP * PSZ * 5 // 8, MAXP * PSZ, 2).astype(jnp.int32)
    queries = draw_queries(jax.random.fold_in(splits[8], 71), 0)
    fresh_entries = gaussian(splits[6], (REQS, 2, KVH, HD), 1.0, 6.0, ((0, 32), (2, 4)))
    out_weight = gaussian(splits[7], (HQ * HD, D), (HQ * HD) ** -0.5, 0.125, ((0, 4),))
    return {"page_cache": page_cache, "keep_list": keep_list, "fold_weight": fold_weight, "page_table": page_table, "lengths": lengths, "queries": queries, "fresh_entries": fresh_entries, "out_weight": out_weight}


negative_floor = -1e30


def compact_page(inputs):
    page, keep_row, weight_row, valid_count = inputs
    slot_index = jnp.arange(PSZ, dtype=jnp.int32)
    valid = slot_index < valid_count
    kept_mask = jnp.logical_and(valid, keep_row > 0)
    dropped = jnp.logical_and(valid, keep_row == 0)
    kept_flag = kept_mask.astype(jnp.int32)
    position = jnp.cumsum(kept_flag) - kept_flag
    total_kept = jnp.sum(kept_flag)
    target = jnp.where(kept_mask, position, PSZ).astype(jnp.int32)
    moved = jnp.zeros_like(page).at[:, :, target, :].set(page, mode="drop")
    dropped_weight = jnp.where(dropped, weight_row, 0.0)
    weight_sum = jnp.sum(dropped_weight)
    folded = jnp.einsum("t,chtd->chd", dropped_weight, page.astype(jnp.float32), precision=lax.Precision.HIGHEST)
    folded = (folded / jnp.maximum(weight_sum, 1.0)).astype(jnp.bfloat16)
    at_fold = slot_index == total_kept
    packed = jnp.where(at_fold[None, None, :, None], folded[:, :, None, :], moved)
    page_mass = jnp.where(slot_index < total_kept, 1.0, jnp.where(at_fold, weight_sum, 0.0)).astype(jnp.bfloat16)
    return packed, page_mass


def reference(page_cache, keep_list, fold_weight, page_table, lengths, queries, fresh_entries, out_weight):
    table_flat = page_table.reshape(-1).astype(jnp.int32)
    logical = jnp.zeros((PAGES,), jnp.int32).at[table_flat].set(jnp.arange(PAGES, dtype=jnp.int32))
    request = logical // MAXP
    within = logical % MAXP
    valid_count = jnp.clip(lengths[request] - within * PSZ, 0, PSZ).astype(jnp.int32)
    packed_cache, packed_mass = lax.map(compact_page, (page_cache, keep_list, fold_weight, valid_count))
    score_scale = HD ** -0.5
    groups = HQ // KVH

    def attend(inputs):
        rows, query_row, fresh = inputs
        pages = packed_cache[rows]
        page_mass = packed_mass[rows].astype(jnp.float32)
        query_f = query_row.astype(jnp.float32).reshape(KVH, groups, HD)
        keys = pages[:, 0].astype(jnp.float32)
        values = pages[:, 1].astype(jnp.float32)
        scores = jnp.einsum("hgd,phtd->phgt", query_f, keys) * score_scale
        live_mask = (page_mass > 0)[:, None, None, :]
        page_top = jnp.max(jnp.where(live_mask, scores, negative_floor), axis=-1)
        weights = jnp.where(live_mask, page_mass[:, None, None, :] * jnp.exp(scores - page_top[..., None]), 0.0)
        page_total = jnp.sum(weights, axis=-1)
        rounded = lax.optimization_barrier(weights.astype(jnp.bfloat16)).astype(jnp.float32)
        page_part = jnp.einsum("phgt,phtd->phgd", rounded, values)
        fresh_key = fresh[0].astype(jnp.float32)
        fresh_value = fresh[1].astype(jnp.float32)
        own_score = jnp.einsum("hgd,hd->hg", query_f, fresh_key) * score_scale
        best_score = jnp.maximum(jnp.max(page_top, axis=0), own_score)
        factor = jnp.exp(page_top - best_score[None])
        own_factor = jnp.exp(own_score - best_score)
        denominator = jnp.sum(factor * page_total, axis=0) + own_factor
        numerator = jnp.sum(factor[..., None] * page_part, axis=0) + own_factor[..., None] * fresh_value[:, None, :]
        return (numerator / denominator[..., None]).astype(jnp.bfloat16).reshape(HQ * HD)

    attended = lax.map(attend, (page_table.astype(jnp.int32), queries, fresh_entries))
    projected = jnp.dot(attended, out_weight, preferred_element_type=jnp.float32).astype(jnp.bfloat16)
    return packed_cache, packed_mass, attended, projected
```

```python
import functools

import jax
import jax.numpy as jnp
from jax import lax
from jax.experimental import pallas as pl
from jax.experimental.pallas import tpu as pltpu
from jax.sharding import PartitionSpec as P

MESH = pl.DeviceIdType.MESH
F32 = jnp.float32
BF16 = jnp.bfloat16
I32 = jnp.int32
floor_value = -1e30
CHUNK = 4


def iota(shape, axis):
    return lax.broadcasted_iota(I32, shape, axis)


def split(x, parts):
    out = []
    for _ in range(parts):
        piece = x.astype(BF16)
        out.append(piece)
        x = x - piece.astype(F32)
    return out


def dot(a, b):
    return jnp.dot(a, b, preferred_element_type=F32)


def dot_nt(a, b):
    return lax.dot_general(a, b, (((1,), (1,)), ((), ())), preferred_element_type=F32)


def one_hot_dot(mask, x, parts):
    sel = mask.astype(F32).astype(BF16)
    return sum(dot(sel, piece) for piece in split(x, parts))


def to_row(col, diag):
    return jnp.sum(jnp.where(diag, col, 0.0), axis=0, keepdims=True)


def main_kernel(
    page_hbm, keep_hbm, weight_hbm, table_hbm, lengths_hbm, query_hbm, fresh_hbm, out_weight_hbm,
    packed_ref, mass_ref, attended_ref, projected_ref,
    pages, keep, weight, table, lengths, query, fresh, out_weight,
    query_flat, fresh_flat, query_send, query_recv, part_send, part_recv, sum_send, sum_recv,
    target_rows, count_rows, fold_rows, divisor_rows, mass_rows, query_rows, score_rows, stat_rows, part_rows,
    page_sem, in_sem, query_sems, part_sems, sum_sems,
):
    kv_count, seq_count = lax.axis_size("kv"), lax.axis_size("seq")
    kv_me, me = lax.axis_index("kv"), lax.axis_index("seq")

    def page_copy(i):
        return pltpu.make_async_copy(
            page_hbm.at[pl.ds(i * CHUNK, CHUNK)], pages.at[pl.ds(i * CHUNK, CHUNK)], page_sem.at[i]
        )

    small = [
        pltpu.make_async_copy(src, dst, in_sem.at[i])
        for i, (src, dst) in enumerate(
            [(table_hbm, table), (query_hbm, query), (lengths_hbm, lengths), (keep_hbm, keep),
             (weight_hbm, weight), (fresh_hbm, fresh), (out_weight_hbm, out_weight)]
        )
    ]
    for copy in small[:6]:
        copy.start()

    barrier = pltpu.get_barrier_semaphore()

    @pl.loop(1, seq_count)
    def _(k):
        pl.semaphore_signal(
            barrier, inc=1, device_id=(kv_me, lax.rem(me + k, seq_count)), device_id_type=MESH
        )

    @pl.loop(1, kv_count)
    def _(k):
        pl.semaphore_signal(
            barrier, inc=1, device_id=(lax.rem(kv_me + k, kv_count), me), device_id_type=MESH
        )

    @pl.loop(0, 64 // CHUNK)
    def _(i):
        page_copy(i).start()

    small[6].start()

    def exchange(send, recv, sems, rows):
        def one(k):
            other = lax.rem(me + k, seq_count)
            return pltpu.make_async_remote_copy(
                src_ref=send.at[other, pl.ds(0, rows)],
                dst_ref=recv.at[me, pl.ds(0, rows)],
                send_sem=sems.at[0],
                recv_sem=sems.at[1],
                device_id=(kv_me, other),
                device_id_type=MESH,
            )

        def every():
            return pltpu.make_async_remote_copy(
                src_ref=send.at[pl.ds(0, seq_count - 1), pl.ds(0, rows)],
                dst_ref=recv.at[pl.ds(0, seq_count - 1), pl.ds(0, rows)],
                send_sem=sems.at[0],
                recv_sem=sems.at[1],
                device_id=(kv_me, me),
                device_id_type=MESH,
            )

        def start():
            pl.loop(1, seq_count)(lambda k: one(k).start())
            recv[me] = send[me]

        return start, every()

    small[0].wait()
    small[1].wait()
    table_t = table[...]
    for r in range(8):
        query_flat[pl.ds(4 * r, 4), :] = query[r].astype(F32)

    lane = iota((64, 128), 1)
    row = iota((64, 128), 0)
    diag = lane == row
    own_pick = (iota((256, 128), 0) == 8 * me + (iota((256, 128), 1) & 7)).astype(F32).astype(BF16)
    keep_lane = (iota((8, 128), 1) >> 3) == iota((8, 128), 0)

    def own_row(x):
        y = dot(x.astype(F32).astype(BF16), own_pick)
        return jnp.sum(jnp.where(keep_lane, y, 0.0), axis=0, keepdims=True)

    holder_row = own_row(table_t >> 6)
    slot_row = own_row(table_t & 63)
    inside = iota((1, 128), 1) < 64
    holder_row = jnp.where(inside, holder_row, -1.0)
    page_row = holder_row * 64.0 + slot_row

    def to_col(x):
        return jnp.sum(jnp.where(diag, x, 0.0), axis=1, keepdims=True)

    earlier = jnp.logical_and(to_col(holder_row) == holder_row, to_col(page_row) < page_row)
    within_row = jnp.sum(earlier.astype(F32), axis=0, keepdims=True)
    entry_row = 2.0 * holder_row + within_row
    slot_of = 2 * (row & 31) + (row >> 5)
    entry_pick = jnp.where(inside, entry_row, -1.0) == slot_of.astype(F32)
    picked = dot(
        entry_pick.astype(F32).astype(BF16),
        jnp.concatenate(
            [
                jnp.concatenate([query_flat[pl.ds(h, 8, stride=4), :].astype(BF16).astype(F32)] * 16, axis=0)
                for h in range(4)
            ],
            axis=1,
        ).astype(BF16),
    )
    for k in range(2):
        for h in range(4):
            query_send.reshape(256, 128)[pl.ds(k * 4 + h, 32, stride=8), :] = picked[
                k * 32 : k * 32 + 32, h * 128 : h * 128 + 128
            ]

    pl.semaphore_wait(barrier, seq_count - 1 + kv_count - 1)
    start_queries, all_queries = exchange(query_send, query_recv, query_sems, 8)
    start_queries()

    small[2].wait()
    lengths_row = jnp.concatenate([lengths[0:1, :], lengths[1:2, :]], axis=1)
    number = iota((8, 256), 0)
    request = iota((8, 256), 1)
    codes = (
        jnp.clip(lengths_row - 128 * number, 0, 128) + 256 * (request >> 3) + 8192 * (request & 7)
    ).astype(F32)
    here = iota((64, 256), 0) + 64 * me
    code = jnp.zeros((64, 256), F32)
    for j in range(8):
        code = code + jnp.where(table_t[j : j + 1, :] == here, codes[j : j + 1, :], 0.0)
    code = jnp.sum(code, axis=1, keepdims=True).astype(I32)
    valid_count = code & 255
    owner = (code >> 8) & 31
    request_col = (code >> 13).astype(F32)
    owner_col = owner.astype(F32)
    owner_row = jnp.where(inside, to_row(owner_col, diag), -1.0)
    same = owner_col == owner_row
    rank_row = jnp.sum(jnp.logical_and(same, row < lane).astype(F32), axis=0, keepdims=True)
    rank_col = jnp.sum(jnp.logical_and(same, lane < row).astype(F32), axis=1, keepdims=True)
    slot_page_row = jnp.where(inside, 2.0 * owner_row + rank_row, -1.0)
    slot_page_col = 2.0 * owner_col + rank_col

    small[3].wait()
    small[4].wait()
    valid = lane < valid_count
    kept = jnp.logical_and(valid, keep[...] > 0)
    dropped = jnp.logical_and(valid, keep[...] == 0)
    kept_flag = kept.astype(F32)
    upper = (iota((128, 128), 0) < iota((128, 128), 1)).astype(F32).astype(BF16)
    position = dot(kept_flag.astype(BF16), upper)
    count = jnp.sum(kept_flag, axis=1, keepdims=True)
    dropped_weight = jnp.where(dropped, weight[...], 0.0)
    weight_sum = jnp.sum(dropped_weight, axis=1, keepdims=True)
    target_rows[...] = jnp.where(kept, position, -1.0)
    count_rows[...] = jnp.broadcast_to(count, (64, 128))
    divisor_rows[...] = jnp.broadcast_to(jnp.maximum(weight_sum, 1.0), (64, 128))
    for i, piece in enumerate(split(dropped_weight, 3)):
        fold_rows[i] = piece.astype(F32)
    lane_f = lane.astype(F32)
    mass = jnp.where(lane_f < count, 1.0, jnp.where(lane_f == count, weight_sum, 0.0)).astype(BF16)
    mass_ref[...] = mass
    mass_rows[...] = mass.astype(F32)

    slots = iota((128, 128), 0).astype(F32)
    extra_row = iota((16, 128), 0)

    def compact(p):
        target = target_rows[pl.ds(p, 1), :]
        picks = jnp.where(slots == target, 1.0, 0.0)
        extra = jnp.where(extra_row == 0, fold_rows[0, pl.ds(p, 1), :], 0.0)
        extra = jnp.where(extra_row == 1, fold_rows[1, pl.ds(p, 1), :], extra)
        extra = jnp.where(extra_row == 2, fold_rows[2, pl.ds(p, 1), :], extra)
        lhs = jnp.concatenate([picks.astype(BF16), extra.astype(BF16)], axis=0)
        page = jnp.concatenate(
            [pages[p, 0, 0], pages[p, 0, 1], pages[p, 1, 0], pages[p, 1, 1]], axis=1
        )
        moved = dot(lhs, page)
        divisor = divisor_rows[pl.ds(p, 1), :]
        folded = jnp.sum(moved[128:136, :], axis=0, keepdims=True)
        at_fold = slots == count_rows[pl.ds(p, 1), :]
        for i in range(4):
            cols = slice(128 * i, 128 * i + 128)
            packed_ref[p, i // 2, i % 2] = jnp.where(
                at_fold, folded[:, cols] / divisor, moved[:128, cols]
            ).astype(BF16)

    @pl.loop(0, 64 // CHUNK)
    def _(i):
        page_copy(i).wait()
        for j in range(CHUNK):
            compact(i * CHUNK + j)

    all_queries.wait_recv()
    query_recv_flat = query_recv.reshape(256, 128)
    page_pick = slot_page_col == (2 * (lane & 31) + (lane >> 5)).astype(F32)
    page_pick = jnp.logical_and(page_pick, lane < 64).astype(F32).astype(BF16)
    sent = jnp.concatenate(
        [
            jnp.concatenate(
                [query_recv_flat[pl.ds(k * 4 + h, 32, stride=8), :] for k in (0, 1, 0, 1)], axis=0
            )
            for h in range(4)
        ],
        axis=1,
    ).astype(BF16)
    page_query = dot(page_pick, sent)
    zeros = jnp.zeros((64, 128), F32)
    for h in range(4):
        for g in range(2):
            query_rows[g, pl.ds(h, 64, stride=8), :] = (
                page_query[:, h * 128 : h * 128 + 128] if g == h // 2 else zeros
            )
            query_rows[g, pl.ds(4 + h, 64, stride=8), :] = zeros

    score_scale = 128 ** -0.5

    @pl.loop(0, 64 // CHUNK)
    def _(i):
        for j in range(CHUNK):
            p = i * CHUNK + j
            keys = jnp.concatenate([packed_ref[p, 0, 0], packed_ref[p, 0, 1]], axis=1)
            q = jnp.concatenate(
                [query_rows[g, pl.ds(pl.multiple_of(p * 8, 8), 8), :] for g in range(2)], axis=1
            ).astype(BF16)
            score_rows[p] = dot_nt(q, keys) * score_scale

    low = iota((8, 128), 0) < 2
    half = iota((8, 128), 1) < 64

    @pl.loop(0, 64 // CHUNK)
    def _(i):
        for j in range(CHUNK):
            p = i * CHUNK + j
            score = score_rows[p]
            page_mass = mass_rows[pl.ds(p, 1), :]
            live = page_mass > 0.0
            top = jnp.max(jnp.where(live, score, floor_value), axis=1, keepdims=True)
            w = jnp.where(live, page_mass * jnp.exp(score - top), 0.0)
            total = jnp.sum(w, axis=1, keepdims=True)
            stat_rows[pl.ds(pl.multiple_of(p * 8, 8), 8), :] = jnp.where(half, top, total)
            values = jnp.concatenate([packed_ref[p, 1, 0], packed_ref[p, 1, 1]], axis=1)
            part = dot(w.astype(BF16), values)
            part_rows[pl.ds(pl.multiple_of(p * 8, 8), 8), :] = jnp.where(low, part[:, :128], part[:, 128:])

    back = slot_page_row == slot_of.astype(F32)
    back = back[:, :64]
    parts = one_hot_dot(
        back, jnp.concatenate([part_rows[pl.ds(h, 64, stride=8), :] for h in range(4)], axis=1), 2
    )
    stats = jnp.where(lane == 8, request_col, 0.0)
    for h in range(4):
        stats = jnp.where((lane & 63) == h, stat_rows[pl.ds(h, 64, stride=8), :], stats)
    stats = one_hot_dot(back, stats, 3)
    part_send_flat = part_send.reshape(512, 128)
    for k in range(2):
        rows = slice(k * 32, k * 32 + 32)
        for h in range(4):
            part_send_flat[pl.ds(k * 4 + h, 32, stride=16), :] = parts[rows, h * 128 : h * 128 + 128]
        part_send_flat[pl.ds(8 + k, 32, stride=16), :] = stats[rows, :]
    start_parts, all_parts = exchange(part_send, part_recv, part_sems, 10)
    start_parts()

    small[5].wait()
    for r in range(8):
        for c in range(2):
            both = fresh[r, c].astype(F32)
            for g in range(2):
                fresh_flat[pl.ds((c * 2 + g) * 8 + r, 1), :] = both[g : g + 1, :]
    lane8 = iota((8, 128), 1)
    own = jnp.zeros((8, 128), F32)
    for h in range(4):
        q = query_flat[pl.ds(h, 8, stride=4), :]
        key = fresh_flat[pl.ds((h // 2) * 8, 8), :]
        own = jnp.where(lane8 == h, jnp.sum(q * key, axis=1, keepdims=True) * score_scale, own)

    all_queries.wait_send()
    all_parts.wait_recv()
    part_recv_flat = part_recv.reshape(512, 128)
    stats = jnp.concatenate(
        [part_recv_flat[pl.ds(8 + k, 32, stride=16), :] for k in range(2)], axis=0
    )
    request_col = jnp.sum(jnp.where(lane == 8, stats, 0.0), axis=1, keepdims=True)
    top = jnp.where(lane < 4, stats, 0.0)
    total = jnp.where(lane < 4, pltpu.roll(stats, 64, 1), 0.0)
    best = own
    for r in range(8):
        one = jnp.max(jnp.where(request_col == float(r), top, floor_value), axis=0, keepdims=True)
        best = jnp.where(jnp.logical_and(iota((8, 128), 0) == r, lane8 < 4), jnp.maximum(best, one), best)
    best_rows = jnp.zeros((64, 128), F32)
    for r in range(8):
        best_rows = jnp.where(request_col == float(r), best[r : r + 1, :], best_rows)
    factor = jnp.exp(top - best_rows)
    gather = iota((8, 128), 0).astype(F32) == jnp.where(inside, to_row(request_col, diag), -1.0)
    scaled = [
        factor[:, h : h + 1]
        * jnp.concatenate(
            [part_recv_flat[pl.ds(k * 4 + h, 32, stride=16), :] for k in range(2)], axis=0
        )
        for h in range(4)
    ]
    sums = one_hot_dot(gather[:, :64], jnp.concatenate(scaled + [factor * total], axis=1), 3)
    own_factor = jnp.exp(own - best)
    denominator = sums[:, 512:] + own_factor
    attended = jnp.concatenate(
        [
            (
                sums[:, h * 128 : h * 128 + 128]
                + own_factor[:, h : h + 1] * fresh_flat[pl.ds(16 + (h // 2) * 8, 8), :]
            )
            / denominator[:, h : h + 1]
            for h in range(4)
        ],
        axis=1,
    ).astype(BF16)
    attended_ref[...] = attended

    small[6].wait()
    for c in range(4):
        sum_send[c] = dot(attended, out_weight[:, c * 512 : c * 512 + 512])

    def sum_copy(k):
        other = lax.rem(kv_me + k, kv_count)
        return pltpu.make_async_remote_copy(
            src_ref=sum_send.at[other],
            dst_ref=sum_recv.at[kv_me],
            send_sem=sum_sems.at[0],
            recv_sem=sum_sems.at[1],
            device_id=(other, me),
            device_id_type=MESH,
        )

    pl.loop(1, kv_count)(lambda k: sum_copy(k).start())
    sum_recv[kv_me] = sum_send[kv_me]
    all_sums = pltpu.make_async_remote_copy(
        src_ref=sum_send.at[pl.ds(0, 3)],
        dst_ref=sum_recv.at[pl.ds(0, 3)],
        send_sem=sum_sems.at[0],
        recv_sem=sum_sems.at[1],
        device_id=(kv_me, me),
        device_id_type=MESH,
    )
    all_parts.wait_send()
    all_sums.wait_recv()
    projected_ref[...] = (sum_recv[0] + sum_recv[1] + sum_recv[2] + sum_recv[3]).astype(BF16)
    all_sums.wait_send()


def write_kernel(*refs):
    n = (len(refs) - 1) // 2
    copies = [pltpu.make_async_copy(refs[i], refs[n + i], refs[-1].at[i]) for i in range(n)]
    for copy in copies:
        copy.start()
    for copy in copies:
        copy.wait()


def per_device(
    page_cache, keep_list, fold_weight, page_table, lengths, queries, fresh_entries, out_weight
):
    anywhere = pl.BlockSpec(memory_space=pl.ANY)
    shapes = [((64, 2, 2, 128, 128), BF16), ((64, 128), BF16), ((8, 512), BF16), ((8, 512), BF16)]
    results = pl.pallas_call(
        main_kernel,
        out_shape=[pltpu.VMEM(shape, dtype) for shape, dtype in shapes],
        in_specs=[anywhere] * 8,
        out_specs=[pl.BlockSpec(memory_space=pltpu.VMEM)] * 4,
        scratch_shapes=[
            pltpu.VMEM((64, 2, 2, 128, 128), BF16),
            pltpu.VMEM((64, 128), I32),
            pltpu.VMEM((64, 128), F32),
            pltpu.VMEM((8, 256), I32),
            pltpu.VMEM((2, 128), I32),
            pltpu.VMEM((8, 4, 128), BF16),
            pltpu.VMEM((8, 2, 2, 128), BF16),
            pltpu.VMEM((512, 2048), BF16),
            pltpu.VMEM((32, 128), F32),
            pltpu.VMEM((32, 128), F32),
            pltpu.VMEM((32, 8, 128), F32),
            pltpu.VMEM((32, 8, 128), F32),
            pltpu.VMEM((32, 16, 128), F32),
            pltpu.VMEM((32, 16, 128), F32),
            pltpu.VMEM((4, 8, 512), F32),
            pltpu.VMEM((4, 8, 512), F32),
            pltpu.VMEM((64, 128), F32),
            pltpu.VMEM((64, 128), F32),
            pltpu.VMEM((3, 64, 128), F32),
            pltpu.VMEM((64, 128), F32),
            pltpu.VMEM((64, 128), F32),
            pltpu.VMEM((2, 512, 128), F32),
            pltpu.VMEM((64, 8, 128), F32),
            pltpu.VMEM((512, 128), F32),
            pltpu.VMEM((512, 128), F32),
            pltpu.SemaphoreType.DMA((64 // CHUNK,)),
            pltpu.SemaphoreType.DMA((7,)),
            pltpu.SemaphoreType.DMA((2,)),
            pltpu.SemaphoreType.DMA((2,)),
            pltpu.SemaphoreType.DMA((2,)),
        ],
        compiler_params=pltpu.CompilerParams(
            collective_id=0, has_side_effects=True, vmem_limit_bytes=36 << 20
        ),
        name="decode",
    )(
        *(
            pltpu.with_memory_space_constraint(x, pltpu.HBM)
            for x in (
                page_cache, keep_list, fold_weight, page_table.T, lengths.reshape(2, 128), queries,
                fresh_entries, out_weight,
            )
        )
    )
    return tuple(
        pl.pallas_call(
            write_kernel,
            out_shape=[jax.ShapeDtypeStruct(shape, dtype) for shape, dtype in shapes],
            in_specs=[anywhere] * 4,
            out_specs=[anywhere] * 4,
            scratch_shapes=[pltpu.SemaphoreType.DMA((4,))],
            compiler_params=pltpu.CompilerParams(vmem_limit_bytes=1 << 20),
            name="write",
        )(*results)
    )


def solution(mesh):
    placed = (
        P("seq", None, "kv", None, None),
        P("seq", None),
        P("seq", None),
        P(),
        P(),
        P("seq", "kv", None),
        P("seq", None, "kv", None),
        P("kv", None),
    )
    return jax.shard_map(
        per_device,
        mesh=mesh,
        in_specs=placed,
        out_specs=(
            P("seq", None, "kv", None, None),
            P("seq", None),
            P("seq", "kv"),
            P("seq", "kv"),
        ),
        check_vma=False,
    )
```

```python
import functools

import jax
import jax.numpy as jnp
from jax import lax
from jax.experimental import pallas as pl
from jax.experimental.pallas import tpu as pltpu
from jax.sharding import PartitionSpec as P

MESH = pl.DeviceIdType.MESH
F32 = jnp.float32
BF16 = jnp.bfloat16
I32 = jnp.int32
floor_value = -1e30
CHUNK = 4
EARLY = 6
GROUP = 4


def iota(shape, axis):
    return lax.broadcasted_iota(I32, shape, axis)


def split(x, parts):
    out = []
    for _ in range(parts):
        piece = x.astype(BF16)
        out.append(piece)
        x = x - piece.astype(F32)
    return out


def dot(a, b):
    return jnp.dot(a, b, preferred_element_type=F32)


def dot_nt(a, b):
    return lax.dot_general(a, b, (((1,), (1,)), ((), ())), preferred_element_type=F32)


def one_hot_dot(mask, x, parts):
    sel = mask.astype(F32).astype(BF16)
    return sum(dot(sel, piece) for piece in split(x, parts))


def to_row(col, diag):
    return jnp.sum(jnp.where(diag, col, 0.0), axis=0, keepdims=True)


def main_kernel(
    page_hbm, keep_hbm, weight_hbm, table_hbm, lengths_hbm, query_hbm, fresh_hbm, out_weight_hbm,
    packed_ref, mass_ref, attended_ref, projected_ref,
    pages, keep, weight, table, lengths, query, fresh, out_weight,
    query_flat, fresh_flat, query_send, query_recv, part_send, part_recv, sum_send, sum_recv,
    target_rows, count_rows, fold_rows, divisor_rows, mass_rows, score_rows, order_vmem, order,
    page_sem, in_sem, query_send_sem, query_recv_sems, part_sems, sum_sems, order_sem,
):
    kv_count, seq_count = lax.axis_size("kv"), lax.axis_size("seq")
    kv_me, me = lax.axis_index("kv"), lax.axis_index("seq")

    def page_copy(i):
        return pltpu.make_async_copy(
            page_hbm.at[pl.ds(i * CHUNK, CHUNK)], pages.at[pl.ds(i * CHUNK, CHUNK)], page_sem.at[i]
        )

    small = [
        pltpu.make_async_copy(src, dst, in_sem.at[i])
        for i, (src, dst) in enumerate(
            [(table_hbm, table), (query_hbm, query), (lengths_hbm, lengths), (keep_hbm, keep),
             (weight_hbm, weight), (fresh_hbm, fresh), (out_weight_hbm, out_weight)]
        )
    ]
    for copy in small[:6]:
        copy.start()

    def at(k):
        return lax.rem(me + k, seq_count)

    barrier = pltpu.get_barrier_semaphore()
    for k in range(1, seq_count):
        pl.semaphore_signal(barrier, inc=1, device_id=(kv_me, at(k)), device_id_type=MESH)
    for k in range(1, kv_count):
        pl.semaphore_signal(
            barrier, inc=1, device_id=(lax.rem(kv_me + k, kv_count), me), device_id_type=MESH
        )

    @pl.loop(0, 64 // CHUNK)
    def _(i):
        page_copy(i).start()

    small[6].start()

    small[0].wait()
    small[1].wait()
    small[2].wait()
    small[3].wait()
    small[4].wait()
    table_t = table[...]
    for r in range(8):
        query_flat[pl.ds(4 * r, 4), :] = query[r].astype(F32)

    lane = iota((64, 128), 1)
    row = iota((64, 128), 0)
    diag = lane == row
    own_pick = (iota((256, 128), 0) == 8 * me + (iota((256, 128), 1) & 7)).astype(F32).astype(BF16)
    keep_lane = (iota((8, 128), 1) >> 3) == iota((8, 128), 0)

    def own_row(x):
        y = dot(x.astype(F32).astype(BF16), own_pick)
        return jnp.sum(jnp.where(keep_lane, y, 0.0), axis=0, keepdims=True)

    inside = iota((1, 128), 1) < 64
    holder_row = jnp.where(inside, own_row(table_t >> 6), -1.0)
    page_row = holder_row * 64.0 + own_row(table_t & 63)

    def to_col(x):
        return jnp.sum(jnp.where(diag, x, 0.0), axis=1, keepdims=True)

    earlier = jnp.logical_and(to_col(holder_row) == holder_row, to_col(page_row) < page_row)
    within_row = jnp.sum(earlier.astype(F32), axis=0, keepdims=True)
    entry_row = jnp.where(inside, 2.0 * holder_row + within_row, -1.0)
    slot_of = (2 * (row & 31) + (row >> 5)).astype(F32)
    entry_pick = (entry_row == slot_of).astype(F32)
    entry_pick_b = entry_pick.astype(BF16)
    picked = dot(
        entry_pick_b,
        jnp.concatenate(
            [jnp.concatenate([query_flat[pl.ds(h, 8, stride=4), :]] * 16, axis=0) for h in range(4)],
            axis=1,
        ).astype(BF16),
    )
    for k in range(2):
        for h in range(4):
            query_send.reshape(256, 128)[pl.ds(k * 4 + h, 32, stride=8), :] = picked[
                k * 32 : k * 32 + 32, h * 128 : h * 128 + 128
            ]
    request_col = jnp.sum(entry_pick * (lane & 7).astype(F32), axis=1, keepdims=True)
    request_is = ((iota((8, 128), 1) & 7) == iota((8, 128), 0)).astype(F32).astype(BF16)
    gather = dot_nt(request_is, entry_pick_b)

    lengths_row = jnp.concatenate([lengths[0:1, :], lengths[1:2, :]], axis=1)
    number = iota((8, 256), 0)
    request = iota((8, 256), 1)
    codes = (jnp.clip(lengths_row - 128 * number, 0, 128) + 256 * (request >> 3)).astype(F32)
    here = iota((64, 256), 0) + 64 * me
    code = jnp.zeros((64, 256), F32)
    for j in range(8):
        code = code + jnp.where(table_t[j : j + 1, :] == here, codes[j : j + 1, :], 0.0)
    code = jnp.sum(code, axis=1, keepdims=True).astype(I32)
    valid_count = code & 255
    owner_col = (code >> 8).astype(F32)
    owner_row = jnp.where(inside, to_row(owner_col, diag), -1.0)
    before = jnp.logical_and(owner_col == owner_row, lane < row)
    slot_col = 2.0 * owner_col + jnp.sum(before.astype(F32), axis=1, keepdims=True)
    order_row = jnp.where(slot_col == lane.astype(F32), row.astype(F32), 0.0)
    order_vmem[...] = jnp.sum(order_row, axis=0, keepdims=True).astype(I32)
    order_copy = pltpu.make_async_copy(order_vmem, order, order_sem)
    order_copy.start()

    valid = lane < valid_count
    kept = jnp.logical_and(valid, keep[...] > 0)
    dropped = jnp.logical_and(valid, keep[...] == 0)
    kept_flag = kept.astype(F32)
    upper = (iota((128, 128), 0) < iota((128, 128), 1)).astype(F32).astype(BF16)
    position = dot(kept_flag.astype(BF16), upper)
    count = jnp.sum(kept_flag, axis=1, keepdims=True)
    dropped_weight = jnp.where(dropped, weight[...], 0.0)
    weight_sum = jnp.sum(dropped_weight, axis=1, keepdims=True)
    target_rows[...] = jnp.where(kept, position, -1.0)
    count_rows[...] = jnp.broadcast_to(count, (64, 128))
    divisor_rows[...] = jnp.broadcast_to(jnp.maximum(weight_sum, 1.0), (64, 128))
    for i, piece in enumerate(split(dropped_weight, 3)):
        fold_rows[i] = piece.astype(F32)
    lane_f = lane.astype(F32)
    mass = jnp.where(lane_f < count, 1.0, jnp.where(lane_f == count, weight_sum, 0.0)).astype(BF16)
    mass_ref[...] = mass
    mass_rows[...] = mass.astype(F32)

    slots = iota((128, 128), 0).astype(F32)
    extra_row = iota((16, 128), 0)

    def compact(p):
        target = target_rows[pl.ds(p, 1), :]
        picks = jnp.where(slots == target, 1.0, 0.0)
        extra = jnp.where(extra_row == 0, fold_rows[0, pl.ds(p, 1), :], 0.0)
        extra = jnp.where(extra_row == 1, fold_rows[1, pl.ds(p, 1), :], extra)
        extra = jnp.where(extra_row == 2, fold_rows[2, pl.ds(p, 1), :], extra)
        lhs = jnp.concatenate([picks.astype(BF16), extra.astype(BF16)], axis=0)
        page = jnp.concatenate(
            [pages[p, 0, 0], pages[p, 0, 1], pages[p, 1, 0], pages[p, 1, 1]], axis=1
        )
        moved = dot(lhs, page)
        divisor = divisor_rows[pl.ds(p, 1), :]
        folded = jnp.sum(moved[128:136, :], axis=0, keepdims=True)
        at_fold = slots == count_rows[pl.ds(p, 1), :]
        for i in range(4):
            cols = slice(128 * i, 128 * i + 128)
            packed_ref[p, i // 2, i % 2] = jnp.where(
                at_fold, folded[:, cols] / divisor, moved[:128, cols]
            ).astype(BF16)

    def query_copy(k):
        other = at(k)
        return pltpu.make_async_remote_copy(
            src_ref=query_send.at[other],
            dst_ref=query_recv.at[me],
            send_sem=query_send_sem,
            recv_sem=query_recv_sems.at[me],
            device_id=(kv_me, other),
            device_id_type=MESH,
        )

    @pl.loop(0, EARLY)
    def _(i):
        page_copy(i).wait()
        for j in range(CHUNK):
            compact(i * CHUNK + j)

    pl.semaphore_wait(barrier, seq_count - 1 + kv_count - 1)
    for k in range(1, seq_count):
        query_copy(k).start()
    query_recv[me] = query_send[me]

    @pl.loop(EARLY, 64 // CHUNK)
    def _(i):
        page_copy(i).wait()
        for j in range(CHUNK):
            compact(i * CHUNK + j)

    small[5].wait()
    for r in range(8):
        for c in range(2):
            both = fresh[r, c].astype(F32)
            for g in range(2):
                fresh_flat[pl.ds((c * 2 + g) * 8 + r, 1), :] = both[g : g + 1, :]
    score_scale = 128 ** -0.5
    lane8 = iota((8, 128), 1)
    row8 = iota((8, 128), 0)
    own = jnp.zeros((8, 128), F32)
    for h in range(4):
        q = query_flat[pl.ds(h, 8, stride=4), :]
        key = fresh_flat[pl.ds((h // 2) * 8, 8), :]
        own = jnp.where(lane8 == h, jnp.sum(q * key, axis=1, keepdims=True) * score_scale, own)

    order_copy.wait()
    first = row8 < 4
    head_low = (row8 & 3) < 2

    def pages_of(o):
        return order[0, 2 * o] & 63, order[0, 2 * o + 1] & 63

    def scores(k):
        o = at(k)
        a, b = pages_of(o)
        q = query_recv[o]
        q = jnp.concatenate(
            [jnp.where(head_low, q, 0.0), jnp.where(head_low, 0.0, q)], axis=1
        ).astype(BF16)
        keys = [jnp.concatenate([packed_ref[p, 0, 0], packed_ref[p, 0, 1]], axis=1) for p in (a, b)]
        score_rows[k - 1] = jnp.where(first, dot_nt(q, keys[0]), dot_nt(q, keys[1])) * score_scale

    def finish(k):
        o = at(k)
        a, b = pages_of(o)
        page_mass = jnp.where(first, mass_rows[pl.ds(a, 1), :], mass_rows[pl.ds(b, 1), :])
        live = page_mass > 0.0
        score = score_rows[k - 1]
        top = jnp.max(jnp.where(live, score, floor_value), axis=1, keepdims=True)
        w = jnp.where(live, page_mass * jnp.exp(score - top), 0.0)
        total = jnp.sum(w, axis=1, keepdims=True)
        w = w.astype(BF16)
        values = [jnp.concatenate([packed_ref[p, 1, 0], packed_ref[p, 1, 1]], axis=1) for p in (a, b)]
        part = jnp.where(jnp.concatenate([first, first], axis=1), dot(w, values[0]), dot(w, values[1]))
        part_send[o, pl.ds(0, 8), :] = jnp.where(head_low, part[:, :128], part[:, 128:])
        stat = jnp.where(lane8 == row8, top, jnp.where(lane8 == row8 + 8, total, 0.0))
        part_send[o, pl.ds(8, 1), :] = jnp.sum(stat, axis=0, keepdims=True)

    def part_copy(k):
        other = at(k)
        return pltpu.make_async_remote_copy(
            src_ref=part_send.at[other, pl.ds(0, 9)],
            dst_ref=part_recv.at[me, pl.ds(0, 9)],
            send_sem=part_sems.at[0],
            recv_sem=part_sems.at[1],
            device_id=(kv_me, other),
            device_id_type=MESH,
        )

    def query_wait(k):
        o = at(k)
        pltpu.make_async_remote_copy(
            src_ref=query_send.at[o],
            dst_ref=query_recv.at[o],
            send_sem=query_send_sem,
            recv_sem=query_recv_sems.at[o],
            device_id=(kv_me, o),
            device_id_type=MESH,
        ).wait_recv()

    def group(i):
        return [seq_count - 1 - GROUP * i - j for j in range(GROUP)]

    last = seq_count // GROUP - 1
    for k in group(0):
        query_wait(k)
    for k in group(0):
        scores(k)

    @pl.loop(1, last)
    def _(i):
        for k in group(i):
            query_wait(k)
        for k in group(i):
            scores(k)
        for k in group(i - 1):
            finish(k)
        for k in group(i - 1):
            part_copy(k).start()

    final = group(last)[:-1]
    for k in final:
        query_wait(k)
    for k in final + [seq_count]:
        scores(k)
    for k in group(last - 1):
        finish(k)
    for k in group(last - 1):
        part_copy(k).start()
    for k in final + [seq_count]:
        finish(k)
    for k in final:
        part_copy(k).start()
    part_recv[me] = part_send[me]

    def all_of(send, recv, send_sem, recv_sem, n, *rest):
        return pltpu.make_async_remote_copy(
            src_ref=send.at[(pl.ds(0, n), *rest)],
            dst_ref=recv.at[(pl.ds(0, n), *rest)],
            send_sem=send_sem,
            recv_sem=recv_sem,
            device_id=(kv_me, me),
            device_id_type=MESH,
        )

    all_parts = all_of(
        part_send, part_recv, part_sems.at[0], part_sems.at[1], seq_count - 1, pl.ds(0, 9)
    )
    all_parts.wait_recv()
    part_recv_flat = part_recv.reshape(512, 128)
    stats = part_recv_flat[pl.ds(8, 32, stride=16), :]
    top = jnp.concatenate([stats, pltpu.roll(stats, 124, 1)], axis=0)
    total = jnp.concatenate([pltpu.roll(stats, 120, 1), pltpu.roll(stats, 116, 1)], axis=0)
    top = jnp.where(lane < 4, top, 0.0)
    total = jnp.where(lane < 4, total, 0.0)
    best = own
    for r in range(8):
        one = jnp.max(jnp.where(request_col == float(r), top, floor_value), axis=0, keepdims=True)
        best = jnp.where(jnp.logical_and(row8 == r, lane8 < 4), jnp.maximum(best, one), best)
    best_rows = jnp.zeros((64, 128), F32)
    for r in range(8):
        best_rows = jnp.where(request_col == float(r), best[r : r + 1, :], best_rows)
    factor = jnp.exp(top - best_rows)
    scaled = [
        factor[:, h : h + 1]
        * jnp.concatenate(
            [part_recv_flat[pl.ds(k * 4 + h, 32, stride=16), :] for k in range(2)], axis=0
        )
        for h in range(4)
    ]
    gather_b = gather.astype(BF16)
    sums = sum(
        dot(gather_b, piece) for piece in split(jnp.concatenate(scaled + [factor * total], axis=1), 3)
    )
    own_factor = jnp.exp(own - best)
    denominator = sums[:, 512:] + own_factor
    attended = jnp.concatenate(
        [
            (
                sums[:, h * 128 : h * 128 + 128]
                + own_factor[:, h : h + 1] * fresh_flat[pl.ds(16 + (h // 2) * 8, 8), :]
            )
            / denominator[:, h : h + 1]
            for h in range(4)
        ],
        axis=1,
    ).astype(BF16)
    attended_ref[...] = attended

    small[6].wait()

    def sum_block(k):
        other = lax.rem(kv_me + k, kv_count)
        return dot(attended, out_weight[:, pl.ds(pl.multiple_of(other * 512, 512), 512)])

    for k in (2, 1, 3):
        other = lax.rem(kv_me + k, kv_count)
        sum_send[other] = sum_block(k).astype(BF16)
        pltpu.make_async_remote_copy(
            src_ref=sum_send.at[other],
            dst_ref=sum_recv.at[k - 1],
            send_sem=sum_sems.at[0],
            recv_sem=sum_sems.at[1],
            device_id=(other, me),
            device_id_type=MESH,
        ).start()
    mine = sum_block(0)
    all_parts.wait_send()
    all_of(query_send, query_recv, query_send_sem, query_recv_sems.at[0], seq_count - 1).wait_send()
    all_sums = all_of(sum_send, sum_recv, sum_sems.at[0], sum_sems.at[1], kv_count - 1)
    all_sums.wait_recv()
    for k in range(3):
        mine = mine + sum_recv[k].astype(F32)
    projected_ref[...] = mine.astype(BF16)
    all_sums.wait_send()


def write_kernel(*refs):
    n = (len(refs) - 1) // 2
    sems = refs[-1]
    copies = [
        pltpu.make_async_copy(
            refs[0].at[pl.ds(i * 8, 8)], refs[n].at[pl.ds(i * 8, 8)], sems.at[n + i]
        )
        for i in range(8)
    ] + [pltpu.make_async_copy(refs[i], refs[n + i], sems.at[i]) for i in range(1, n)]
    for copy in copies:
        copy.start()
    for copy in copies:
        copy.wait()


def per_device(
    page_cache, keep_list, fold_weight, page_table, lengths, queries, fresh_entries, out_weight
):
    anywhere = pl.BlockSpec(memory_space=pl.ANY)
    shapes = [((64, 2, 2, 128, 128), BF16), ((64, 128), BF16), ((8, 512), BF16), ((8, 512), BF16)]
    results = pl.pallas_call(
        main_kernel,
        out_shape=[pltpu.VMEM(shape, dtype) for shape, dtype in shapes],
        in_specs=[anywhere] * 8,
        out_specs=[pl.BlockSpec(memory_space=pltpu.VMEM)] * 4,
        scratch_shapes=[
            pltpu.VMEM((64, 2, 2, 128, 128), BF16),
            pltpu.VMEM((64, 128), I32),
            pltpu.VMEM((64, 128), F32),
            pltpu.VMEM((8, 256), I32),
            pltpu.VMEM((2, 128), I32),
            pltpu.VMEM((8, 4, 128), BF16),
            pltpu.VMEM((8, 2, 2, 128), BF16),
            pltpu.VMEM((512, 2048), BF16),
            pltpu.VMEM((32, 128), F32),
            pltpu.VMEM((32, 128), F32),
            pltpu.VMEM((32, 8, 128), F32),
            pltpu.VMEM((32, 8, 128), F32),
            pltpu.VMEM((32, 16, 128), F32),
            pltpu.VMEM((32, 16, 128), F32),
            pltpu.VMEM((4, 8, 512), BF16),
            pltpu.VMEM((4, 8, 512), BF16),
            pltpu.VMEM((64, 128), F32),
            pltpu.VMEM((64, 128), F32),
            pltpu.VMEM((3, 64, 128), F32),
            pltpu.VMEM((64, 128), F32),
            pltpu.VMEM((64, 128), F32),
            pltpu.VMEM((32, 8, 128), F32),
            pltpu.VMEM((1, 128), I32),
            pltpu.SMEM((1, 128), I32),
            pltpu.SemaphoreType.DMA((64 // CHUNK,)),
            pltpu.SemaphoreType.DMA((7,)),
            pltpu.SemaphoreType.DMA,
            pltpu.SemaphoreType.DMA((32,)),
            pltpu.SemaphoreType.DMA((2,)),
            pltpu.SemaphoreType.DMA((2,)),
            pltpu.SemaphoreType.DMA,
        ],
        compiler_params=pltpu.CompilerParams(
            collective_id=0, has_side_effects=True, vmem_limit_bytes=36 << 20
        ),
        name="decode",
    )(
        *(
            pltpu.with_memory_space_constraint(x, pltpu.HBM)
            for x in (
                page_cache, keep_list, fold_weight, page_table.T, lengths.reshape(2, 128), queries,
                fresh_entries, out_weight,
            )
        )
    )
    return tuple(
        pl.pallas_call(
            write_kernel,
            out_shape=[jax.ShapeDtypeStruct(shape, dtype) for shape, dtype in shapes],
            in_specs=[anywhere] * 4,
            out_specs=[anywhere] * 4,
            scratch_shapes=[pltpu.SemaphoreType.DMA((12,))],
            compiler_params=pltpu.CompilerParams(vmem_limit_bytes=1 << 20),
            name="write",
        )(*results)
    )


def solution(mesh):
    placed = (
        P("seq", None, "kv", None, None),
        P("seq", None),
        P("seq", None),
        P(),
        P(),
        P("seq", "kv", None),
        P("seq", None, "kv", None),
        P("kv", None),
    )
    return jax.shard_map(
        per_device,
        mesh=mesh,
        in_specs=placed,
        out_specs=(
            P("seq", None, "kv", None, None),
            P("seq", None),
            P("seq", "kv"),
            P("seq", "kv"),
        ),
        check_vma=False,
    )
```

```python
import functools

import jax
import jax.numpy as jnp
from jax import lax
from jax.experimental import pallas as pl
from jax.experimental.pallas import tpu as pltpu
from jax.sharding import PartitionSpec as P

MESH = pl.DeviceIdType.MESH
F32 = jnp.float32
BF16 = jnp.bfloat16
I32 = jnp.int32
floor_value = -1e30
CHUNK = 16
GROUP = 16


def iota(shape, axis):
    return lax.broadcasted_iota(I32, shape, axis)


def split(x, parts):
    out = []
    for _ in range(parts):
        piece = x.astype(BF16)
        out.append(piece)
        x = x - piece.astype(F32)
    return out


def dot(a, b):
    return jnp.dot(a, b, preferred_element_type=F32)


def dot_nt(a, b):
    return lax.dot_general(a, b, (((1,), (1,)), ((), ())), preferred_element_type=F32)


def one_hot_dot(mask, x, parts):
    sel = mask.astype(F32).astype(BF16)
    return sum(dot(sel, piece) for piece in split(x, parts))


def to_row(col, diag):
    return jnp.sum(jnp.where(diag, col, 0.0), axis=0, keepdims=True)


def main_kernel(
    page_hbm, keep_hbm, weight_hbm, table_hbm, lengths_hbm, query_hbm, fresh_hbm, out_weight_hbm,
    packed_ref, mass_ref, attended_ref, projected_ref,
    pages, keep, weight, table, lengths, query, fresh, out_weight,
    query_flat, fresh_flat, query_send, query_recv, part_send, part_recv, sum_send, sum_recv,
    target_rows, count_rows, fold_rows, divisor_rows, mass_rows, score_rows, order_vmem, order,
    page_sem, in_sem, query_send_sem, query_recv_sems, part_sems, sum_sems, order_sem,
):
    kv_count, seq_count = lax.axis_size("kv"), lax.axis_size("seq")
    kv_me, me = lax.axis_index("kv"), lax.axis_index("seq")

    def page_copy(i):
        return pltpu.make_async_copy(
            page_hbm.at[pl.ds(i * CHUNK, CHUNK)], pages.at[pl.ds(i * CHUNK, CHUNK)], page_sem.at[i]
        )

    small = [
        pltpu.make_async_copy(src, dst, in_sem.at[i])
        for i, (src, dst) in enumerate(
            [(table_hbm, table), (query_hbm, query), (lengths_hbm, lengths), (keep_hbm, keep),
             (weight_hbm, weight), (fresh_hbm, fresh), (out_weight_hbm, out_weight)]
        )
    ]
    for copy in small[:5]:
        copy.start()

    @pl.loop(0, 64 // CHUNK)
    def _(i):
        page_copy(i).start()

    def at(k):
        return lax.rem(me + k, seq_count)

    barrier = pltpu.get_barrier_semaphore()
    for k in range(1, seq_count):
        pl.semaphore_signal(barrier, inc=1, device_id=(kv_me, at(k)), device_id_type=MESH)
    for k in range(1, kv_count):
        pl.semaphore_signal(
            barrier, inc=1, device_id=(lax.rem(kv_me + k, kv_count), me), device_id_type=MESH
        )

    small[5].start()
    small[6].start()

    small[0].wait()
    small[1].wait()
    table_t = table[...]
    for r in range(8):
        query_flat[pl.ds(4 * r, 4), :] = query[r].astype(F32)

    lane = iota((64, 128), 1)
    row = iota((64, 128), 0)
    diag = lane == row
    own_pick = (iota((256, 128), 0) == 8 * me + (iota((256, 128), 1) & 7)).astype(F32).astype(BF16)
    keep_lane = (iota((8, 128), 1) >> 3) == iota((8, 128), 0)

    def own_row(x):
        y = dot(x.astype(F32).astype(BF16), own_pick)
        return jnp.sum(jnp.where(keep_lane, y, 0.0), axis=0, keepdims=True)

    inside = iota((1, 128), 1) < 64
    holder_row = jnp.where(inside, own_row(table_t >> 6), -1.0)
    page_row = holder_row * 64.0 + own_row(table_t & 63)

    def to_col(x):
        return jnp.sum(jnp.where(diag, x, 0.0), axis=1, keepdims=True)

    earlier = jnp.logical_and(to_col(holder_row) == holder_row, to_col(page_row) < page_row)
    within_row = jnp.sum(earlier.astype(F32), axis=0, keepdims=True)
    entry_row = jnp.where(inside, 2.0 * holder_row + within_row, -1.0)
    slot_of = (2 * (row & 31) + (row >> 5)).astype(F32)
    entry_pick = (entry_row == slot_of).astype(F32)
    entry_pick_b = entry_pick.astype(BF16)
    picked = dot(
        entry_pick_b,
        jnp.concatenate(
            [jnp.concatenate([query_flat[pl.ds(h, 8, stride=4), :]] * 16, axis=0) for h in range(4)],
            axis=1,
        ).astype(BF16),
    )
    for k in range(2):
        for h in range(4):
            query_send.reshape(256, 128)[pl.ds(k * 4 + h, 32, stride=8), :] = picked[
                k * 32 : k * 32 + 32, h * 128 : h * 128 + 128
            ]
    def query_copy(k):
        other = at(k)
        return pltpu.make_async_remote_copy(
            src_ref=query_send.at[other],
            dst_ref=query_recv.at[me],
            send_sem=query_send_sem,
            recv_sem=query_recv_sems.at[me],
            device_id=(kv_me, other),
            device_id_type=MESH,
        )

    pl.semaphore_wait(barrier, seq_count - 1 + kv_count - 1)
    for k in range(1, seq_count):
        query_copy(k).start()
    query_recv[me] = query_send[me]

    request_col = jnp.sum(entry_pick * (lane & 7).astype(F32), axis=1, keepdims=True)
    request_is = ((iota((8, 128), 1) & 7) == iota((8, 128), 0)).astype(F32).astype(BF16)
    gather = dot_nt(request_is, entry_pick_b)

    small[2].wait()
    lengths_row = jnp.concatenate([lengths[0:1, :], lengths[1:2, :]], axis=1)
    number = iota((8, 256), 0)
    request = iota((8, 256), 1)
    codes = (jnp.clip(lengths_row - 128 * number, 0, 128) + 256 * (request >> 3)).astype(F32)
    here = iota((64, 256), 0) + 64 * me
    code = jnp.zeros((64, 256), F32)
    for j in range(8):
        code = code + jnp.where(table_t[j : j + 1, :] == here, codes[j : j + 1, :], 0.0)
    code = jnp.sum(code, axis=1, keepdims=True).astype(I32)
    valid_count = code & 255
    owner_col = (code >> 8).astype(F32)
    owner_row = jnp.where(inside, to_row(owner_col, diag), -1.0)
    before = jnp.logical_and(owner_col == owner_row, lane < row)
    slot_col = 2.0 * owner_col + jnp.sum(before.astype(F32), axis=1, keepdims=True)
    order_row = jnp.where(slot_col == lane.astype(F32), row.astype(F32), 0.0)
    order_vmem[...] = jnp.sum(order_row, axis=0, keepdims=True).astype(I32)
    order_copy = pltpu.make_async_copy(order_vmem, order, order_sem)
    order_copy.start()

    small[3].wait()
    small[4].wait()
    valid = lane < valid_count
    kept = jnp.logical_and(valid, keep[...] > 0)
    dropped = jnp.logical_and(valid, keep[...] == 0)
    kept_flag = kept.astype(F32)
    upper = (iota((128, 128), 0) < iota((128, 128), 1)).astype(F32).astype(BF16)
    position = dot(kept_flag.astype(BF16), upper)
    count = jnp.sum(kept_flag, axis=1, keepdims=True)
    dropped_weight = jnp.where(dropped, weight[...], 0.0)
    weight_sum = jnp.sum(dropped_weight, axis=1, keepdims=True)
    target_rows[...] = jnp.where(kept, position, -1.0)
    count_rows[...] = jnp.broadcast_to(count, (64, 128))
    divisor_rows[...] = jnp.broadcast_to(jnp.maximum(weight_sum, 1.0), (64, 128))
    for i, piece in enumerate(split(dropped_weight, 3)):
        fold_rows[i] = piece.astype(F32)
    lane_f = lane.astype(F32)
    mass = jnp.where(lane_f < count, 1.0, jnp.where(lane_f == count, weight_sum, 0.0)).astype(BF16)
    mass_ref[...] = mass
    mass_rows[...] = mass.astype(F32)

    slots = iota((128, 128), 0).astype(F32)
    extra_row = iota((16, 128), 0)

    def compact(p):
        target = target_rows[pl.ds(p, 1), :]
        picks = jnp.where(slots == target, 1.0, 0.0)
        extra = jnp.where(extra_row == 0, fold_rows[0, pl.ds(p, 1), :], 0.0)
        extra = jnp.where(extra_row == 1, fold_rows[1, pl.ds(p, 1), :], extra)
        extra = jnp.where(extra_row == 2, fold_rows[2, pl.ds(p, 1), :], extra)
        lhs = jnp.concatenate([picks.astype(BF16), extra.astype(BF16)], axis=0)
        page = jnp.concatenate(
            [pages[p, 0, 0], pages[p, 0, 1], pages[p, 1, 0], pages[p, 1, 1]], axis=1
        )
        moved = dot(lhs, page)
        divisor = divisor_rows[pl.ds(p, 1), :]
        folded = jnp.sum(moved[128:136, :], axis=0, keepdims=True)
        at_fold = slots == count_rows[pl.ds(p, 1), :]
        for i in range(4):
            cols = slice(128 * i, 128 * i + 128)
            packed_ref[p, i // 2, i % 2] = jnp.where(
                at_fold, folded[:, cols] / divisor, moved[:128, cols]
            ).astype(BF16)

    @pl.loop(0, 64 // CHUNK)
    def _(i):
        page_copy(i).wait()
        for j in range(CHUNK):
            compact(i * CHUNK + j)

    small[5].wait()
    for r in range(8):
        for c in range(2):
            both = fresh[r, c].astype(F32)
            for g in range(2):
                fresh_flat[pl.ds((c * 2 + g) * 8 + r, 1), :] = both[g : g + 1, :]
    score_scale = 128 ** -0.5
    lane8 = iota((8, 128), 1)
    row8 = iota((8, 128), 0)
    own = jnp.zeros((8, 128), F32)
    for h in range(4):
        q = query_flat[pl.ds(h, 8, stride=4), :]
        key = fresh_flat[pl.ds((h // 2) * 8, 8), :]
        own = jnp.where(lane8 == h, jnp.sum(q * key, axis=1, keepdims=True) * score_scale, own)

    order_copy.wait()
    first = row8 < 4
    head_low = (row8 & 3) < 2

    def pages_of(o):
        return order[0, 2 * o] & 63, order[0, 2 * o + 1] & 63

    def scores(k):
        o = at(k)
        a, b = pages_of(o)
        q = query_recv[o]
        q = jnp.concatenate(
            [jnp.where(head_low, q, 0.0), jnp.where(head_low, 0.0, q)], axis=1
        ).astype(BF16)
        keys = [jnp.concatenate([packed_ref[p, 0, 0], packed_ref[p, 0, 1]], axis=1) for p in (a, b)]
        score_rows[k - 1] = jnp.where(first, dot_nt(q, keys[0]), dot_nt(q, keys[1])) * score_scale

    def finish(k):
        o = at(k)
        a, b = pages_of(o)
        page_mass = jnp.where(first, mass_rows[pl.ds(a, 1), :], mass_rows[pl.ds(b, 1), :])
        live = page_mass > 0.0
        score = score_rows[k - 1]
        top = jnp.max(jnp.where(live, score, floor_value), axis=1, keepdims=True)
        w = jnp.where(live, page_mass * jnp.exp(score - top), 0.0)
        total = jnp.sum(w, axis=1, keepdims=True)
        w = w.astype(BF16)
        values = [jnp.concatenate([packed_ref[p, 1, 0], packed_ref[p, 1, 1]], axis=1) for p in (a, b)]
        part = jnp.where(jnp.concatenate([first, first], axis=1), dot(w, values[0]), dot(w, values[1]))
        part_send[o, pl.ds(0, 8), :] = jnp.where(head_low, part[:, :128], part[:, 128:])
        stat = jnp.where(lane8 == row8, top, jnp.where(lane8 == row8 + 8, total, 0.0))
        part_send[o, pl.ds(8, 1), :] = jnp.sum(stat, axis=0, keepdims=True)

    def part_copy(k):
        other = at(k)
        return pltpu.make_async_remote_copy(
            src_ref=part_send.at[other, pl.ds(0, 9)],
            dst_ref=part_recv.at[me, pl.ds(0, 9)],
            send_sem=part_sems.at[0],
            recv_sem=part_sems.at[1],
            device_id=(kv_me, other),
            device_id_type=MESH,
        )

    def query_wait(k):
        o = at(k)
        pltpu.make_async_remote_copy(
            src_ref=query_send.at[o],
            dst_ref=query_recv.at[o],
            send_sem=query_send_sem,
            recv_sem=query_recv_sems.at[o],
            device_id=(kv_me, o),
            device_id_type=MESH,
        ).wait_recv()

    def group(i):
        return [seq_count - 1 - GROUP * i - j for j in range(GROUP)]

    last = seq_count // GROUP - 1
    for k in group(0):
        query_wait(k)
    for k in group(0):
        scores(k)

    @pl.loop(1, last)
    def _(i):
        for k in group(i):
            query_wait(k)
        for k in group(i):
            scores(k)
        for k in group(i - 1):
            finish(k)
        for k in group(i - 1):
            part_copy(k).start()

    final = group(last)[:-1]
    for k in final:
        query_wait(k)
    for k in final + [seq_count]:
        scores(k)
    for k in group(last - 1):
        finish(k)
    for k in group(last - 1):
        part_copy(k).start()
    for k in final + [seq_count]:
        finish(k)
    for k in final:
        part_copy(k).start()
    part_recv[me] = part_send[me]

    def all_of(send, recv, send_sem, recv_sem, n, *rest):
        return pltpu.make_async_remote_copy(
            src_ref=send.at[(pl.ds(0, n), *rest)],
            dst_ref=recv.at[(pl.ds(0, n), *rest)],
            send_sem=send_sem,
            recv_sem=recv_sem,
            device_id=(kv_me, me),
            device_id_type=MESH,
        )

    all_parts = all_of(
        part_send, part_recv, part_sems.at[0], part_sems.at[1], seq_count - 1, pl.ds(0, 9)
    )
    all_parts.wait_recv()
    part_recv_flat = part_recv.reshape(512, 128)
    stats = part_recv_flat[pl.ds(8, 32, stride=16), :]
    top = jnp.concatenate([stats, pltpu.roll(stats, 124, 1)], axis=0)
    total = jnp.concatenate([pltpu.roll(stats, 120, 1), pltpu.roll(stats, 116, 1)], axis=0)
    top = jnp.where(lane < 4, top, 0.0)
    total = jnp.where(lane < 4, total, 0.0)
    best = own
    for r in range(8):
        one = jnp.max(jnp.where(request_col == float(r), top, floor_value), axis=0, keepdims=True)
        best = jnp.where(jnp.logical_and(row8 == r, lane8 < 4), jnp.maximum(best, one), best)
    best_rows = jnp.zeros((64, 128), F32)
    for r in range(8):
        best_rows = jnp.where(request_col == float(r), best[r : r + 1, :], best_rows)
    factor = jnp.exp(top - best_rows)
    scaled = [
        factor[:, h : h + 1]
        * jnp.concatenate(
            [part_recv_flat[pl.ds(k * 4 + h, 32, stride=16), :] for k in range(2)], axis=0
        )
        for h in range(4)
    ]
    gather_b = gather.astype(BF16)
    sums = sum(
        dot(gather_b, piece) for piece in split(jnp.concatenate(scaled + [factor * total], axis=1), 3)
    )
    own_factor = jnp.exp(own - best)
    denominator = sums[:, 512:] + own_factor
    attended = jnp.concatenate(
        [
            (
                sums[:, h * 128 : h * 128 + 128]
                + own_factor[:, h : h + 1] * fresh_flat[pl.ds(16 + (h // 2) * 8, 8), :]
            )
            / denominator[:, h : h + 1]
            for h in range(4)
        ],
        axis=1,
    ).astype(BF16)
    attended_ref[...] = attended

    small[6].wait()

    def sum_block(k):
        other = lax.rem(kv_me + k, kv_count)
        return dot(attended, out_weight[:, pl.ds(pl.multiple_of(other * 512, 512), 512)])

    for k in (2, 1, 3):
        other = lax.rem(kv_me + k, kv_count)
        sum_send[other] = sum_block(k).astype(BF16)
        pltpu.make_async_remote_copy(
            src_ref=sum_send.at[other],
            dst_ref=sum_recv.at[k - 1],
            send_sem=sum_sems.at[0],
            recv_sem=sum_sems.at[1],
            device_id=(other, me),
            device_id_type=MESH,
        ).start()
    mine = sum_block(0)
    all_parts.wait_send()
    all_of(query_send, query_recv, query_send_sem, query_recv_sems.at[0], seq_count - 1).wait_send()
    all_sums = all_of(sum_send, sum_recv, sum_sems.at[0], sum_sems.at[1], kv_count - 1)
    all_sums.wait_recv()
    for k in range(3):
        mine = mine + sum_recv[k].astype(F32)
    projected_ref[...] = mine.astype(BF16)
    all_sums.wait_send()


def write_kernel(*refs):
    n = (len(refs) - 1) // 2
    sems = refs[-1]
    copies = [
        pltpu.make_async_copy(
            refs[0].at[pl.ds(i * 8, 8)], refs[n].at[pl.ds(i * 8, 8)], sems.at[n + i]
        )
        for i in range(8)
    ] + [pltpu.make_async_copy(refs[i], refs[n + i], sems.at[i]) for i in range(1, n)]
    for copy in copies:
        copy.start()
    for copy in copies:
        copy.wait()


def per_device(
    page_cache, keep_list, fold_weight, page_table, lengths, queries, fresh_entries, out_weight
):
    anywhere = pl.BlockSpec(memory_space=pl.ANY)
    shapes = [((64, 2, 2, 128, 128), BF16), ((64, 128), BF16), ((8, 512), BF16), ((8, 512), BF16)]
    results = pl.pallas_call(
        main_kernel,
        out_shape=[pltpu.VMEM(shape, dtype) for shape, dtype in shapes],
        in_specs=[anywhere] * 8,
        out_specs=[pl.BlockSpec(memory_space=pltpu.VMEM)] * 4,
        scratch_shapes=[
            pltpu.VMEM((64, 2, 2, 128, 128), BF16),
            pltpu.VMEM((64, 128), I32),
            pltpu.VMEM((64, 128), F32),
            pltpu.VMEM((8, 256), I32),
            pltpu.VMEM((2, 128), I32),
            pltpu.VMEM((8, 4, 128), BF16),
            pltpu.VMEM((8, 2, 2, 128), BF16),
            pltpu.VMEM((512, 2048), BF16),
            pltpu.VMEM((32, 128), F32),
            pltpu.VMEM((32, 128), F32),
            pltpu.VMEM((32, 8, 128), F32),
            pltpu.VMEM((32, 8, 128), F32),
            pltpu.VMEM((32, 16, 128), F32),
            pltpu.VMEM((32, 16, 128), F32),
            pltpu.VMEM((4, 8, 512), BF16),
            pltpu.VMEM((4, 8, 512), BF16),
            pltpu.VMEM((64, 128), F32),
            pltpu.VMEM((64, 128), F32),
            pltpu.VMEM((3, 64, 128), F32),
            pltpu.VMEM((64, 128), F32),
            pltpu.VMEM((64, 128), F32),
            pltpu.VMEM((32, 8, 128), F32),
            pltpu.VMEM((1, 128), I32),
            pltpu.SMEM((1, 128), I32),
            pltpu.SemaphoreType.DMA((64 // CHUNK,)),
            pltpu.SemaphoreType.DMA((7,)),
            pltpu.SemaphoreType.DMA,
            pltpu.SemaphoreType.DMA((32,)),
            pltpu.SemaphoreType.DMA((2,)),
            pltpu.SemaphoreType.DMA((2,)),
            pltpu.SemaphoreType.DMA,
        ],
        compiler_params=pltpu.CompilerParams(
            collective_id=0, has_side_effects=True, vmem_limit_bytes=36 << 20
        ),
        name="decode",
    )(
        *(
            pltpu.with_memory_space_constraint(x, pltpu.HBM)
            for x in (
                page_cache, keep_list, fold_weight, page_table.T, lengths.reshape(2, 128), queries,
                fresh_entries, out_weight,
            )
        )
    )
    return tuple(
        pl.pallas_call(
            write_kernel,
            out_shape=[jax.ShapeDtypeStruct(shape, dtype) for shape, dtype in shapes],
            in_specs=[anywhere] * 4,
            out_specs=[anywhere] * 4,
            scratch_shapes=[pltpu.SemaphoreType.DMA((12,))],
            compiler_params=pltpu.CompilerParams(vmem_limit_bytes=1 << 20),
            name="write",
        )(*results)
    )


def solution(mesh):
    placed = (
        P("seq", None, "kv", None, None),
        P("seq", None),
        P("seq", None),
        P(),
        P(),
        P("seq", "kv", None),
        P("seq", None, "kv", None),
        P("kv", None),
    )
    return jax.shard_map(
        per_device,
        mesh=mesh,
        in_specs=placed,
        out_specs=(
            P("seq", None, "kv", None, None),
            P("seq", None),
            P("seq", "kv"),
            P("seq", "kv"),
        ),
        check_vma=False,
    )
```

```python
import functools

import jax
import jax.numpy as jnp
from jax import lax
from jax.experimental import pallas as pl
from jax.experimental.pallas import tpu as pltpu
from jax.sharding import PartitionSpec as P

MESH = pl.DeviceIdType.MESH
F32 = jnp.float32
BF16 = jnp.bfloat16
I32 = jnp.int32
floor_value = -1e30
CHUNK = 16
LEAD = 32
GROUP = 16
PEERS = sorted(
    ((dz, dx, dc) for dz in range(4) for dx in range(4) for dc in range(2)),
    key=lambda d: (-min(d[0], 4 - d[0]) - min(d[1], 4 - d[1]), -d[2], d),
)


def iota(shape, axis):
    return lax.broadcasted_iota(I32, shape, axis)


def split(x, parts):
    out = []
    for _ in range(parts):
        piece = x.astype(BF16)
        out.append(piece)
        x = x - piece.astype(F32)
    return out


def dot(a, b):
    return jnp.dot(a, b, preferred_element_type=F32)


def dot_nt(a, b):
    return lax.dot_general(a, b, (((1,), (1,)), ((), ())), preferred_element_type=F32)


def one_hot_dot(mask, x, parts):
    sel = mask.astype(F32).astype(BF16)
    return sum(dot(sel, piece) for piece in split(x, parts))


def to_row(col, diag):
    return jnp.sum(jnp.where(diag, col, 0.0), axis=0, keepdims=True)


def place_pages(table_t, lengths, me):
    lengths_row = jnp.concatenate([lengths[0:1, :], lengths[1:2, :]], axis=1)
    number = iota((8, 256), 0)
    request = iota((8, 256), 1)
    codes = (jnp.clip(lengths_row - 128 * number, 0, 128) + 256 * (request >> 3)).astype(F32)
    here = iota((64, 256), 0) + 64 * me
    code = jnp.zeros((64, 256), F32)
    for j in range(8):
        code = code + jnp.where(table_t[j : j + 1, :] == here, codes[j : j + 1, :], 0.0)
    code = jnp.sum(code, axis=1, keepdims=True).astype(I32)
    return code & 255, code >> 8


def plan_pages(valid_count, keep, weight, rows):
    target_rows, count_rows, divisor_rows, fold_rows = rows
    lane = iota((64, 128), 1)
    valid = lane < valid_count
    kept = jnp.logical_and(valid, keep[...] > 0)
    dropped = jnp.logical_and(valid, keep[...] == 0)
    kept_flag = kept.astype(F32)
    upper = (iota((128, 128), 0) < iota((128, 128), 1)).astype(F32).astype(BF16)
    position = dot(kept_flag.astype(BF16), upper)
    count = jnp.sum(kept_flag, axis=1, keepdims=True)
    dropped_weight = jnp.where(dropped, weight[...], 0.0)
    weight_sum = jnp.sum(dropped_weight, axis=1, keepdims=True)
    target_rows[...] = jnp.where(kept, position, -1.0)
    count_rows[...] = jnp.broadcast_to(count, (64, 128))
    divisor_rows[...] = jnp.broadcast_to(jnp.maximum(weight_sum, 1.0), (64, 128))
    for i, piece in enumerate(split(dropped_weight, 3)):
        fold_rows[i] = piece.astype(F32)
    lane_f = lane.astype(F32)
    mass = jnp.where(lane_f < count, 1.0, jnp.where(lane_f == count, weight_sum, 0.0)).astype(BF16)
    return mass


def compact_page(p, pages, packed_ref, rows):
    target_rows, count_rows, divisor_rows, fold_rows = rows
    slots = iota((128, 128), 0).astype(F32)
    extra_row = iota((16, 128), 0)
    target = target_rows[pl.ds(p, 1), :]
    picks = jnp.where(slots == target, 1.0, 0.0)
    extra = jnp.where(extra_row == 0, fold_rows[0, pl.ds(p, 1), :], 0.0)
    extra = jnp.where(extra_row == 1, fold_rows[1, pl.ds(p, 1), :], extra)
    extra = jnp.where(extra_row == 2, fold_rows[2, pl.ds(p, 1), :], extra)
    lhs = jnp.concatenate([picks.astype(BF16), extra.astype(BF16)], axis=0)
    page = jnp.concatenate(
        [pages[p, 0, 0], pages[p, 0, 1], pages[p, 1, 0], pages[p, 1, 1]], axis=1
    )
    moved = dot(lhs, page)
    divisor = divisor_rows[pl.ds(p, 1), :]
    folded = jnp.sum(moved[128:136, :], axis=0, keepdims=True)
    at_fold = slots == count_rows[pl.ds(p, 1), :]
    for i in range(4):
        cols = slice(128 * i, 128 * i + 128)
        packed_ref[p, i // 2, i % 2] = jnp.where(
            at_fold, folded[:, cols] / divisor, moved[:128, cols]
        ).astype(BF16)


def share():
    kv_me, me = lax.axis_index("kv"), lax.axis_index("seq")

    def pick(i, values):
        out = values[-1]
        for at in range(len(values) - 1):
            out = jnp.where(i == at, values[at], out)
        return out

    lead = (
        pick(kv_me, (0, 11, 18, 21))
        + pick(me // 8, (0, 13, 27, 29))
        + pick(lax.rem(me // 2, 4), (0, 9, 13, 12))
        + 8 * lax.rem(me, 2)
    )
    return jnp.clip((LEAD - lead + 3) // 4, 0, 8)


def main_kernel(
    page_hbm, keep_hbm, weight_hbm, table_hbm, lengths_hbm, query_hbm, fresh_hbm, out_weight_hbm,
    early,
    packed_ref, mass_ref, attended_ref, projected_ref,
    pages, keep, weight, table, lengths, query, fresh, out_weight,
    query_flat, fresh_flat, query_send, query_recv, part_send, part_recv, sum_send, sum_recv,
    target_rows, count_rows, fold_rows, divisor_rows, mass_rows, score_rows, order_vmem, order,
    page_sem, in_sem, query_send_sem, query_recv_sems, part_sems, sum_sems, order_sem,
):
    kv_count, seq_count = lax.axis_size("kv"), lax.axis_size("seq")
    kv_me, me = lax.axis_index("kv"), lax.axis_index("seq")

    def page_copy(i):
        return pltpu.make_async_copy(
            page_hbm.at[pl.ds(i * CHUNK, CHUNK)], pages.at[pl.ds(i * CHUNK, CHUNK)], page_sem.at[i]
        )

    small = [
        pltpu.make_async_copy(src, dst, in_sem.at[i])
        for i, (src, dst) in enumerate(
            [(table_hbm, table), (query_hbm, query), (lengths_hbm, lengths), (keep_hbm, keep),
             (weight_hbm, weight), (fresh_hbm, fresh), (out_weight_hbm, out_weight)]
        )
    ]
    for copy in small[:5]:
        copy.start()

    @pl.loop(0, 64 // CHUNK)
    def _(i):
        page_copy(i).start()

    where_z, where_x, where_core = me // 8, lax.rem(me // 2, 4), lax.rem(me, 2)

    def at(k):
        dz, dx, dc = PEERS[k - 1]
        return (
            lax.rem(where_z + dz, 4) * 8 + lax.rem(where_x + dx, 4) * 2 + lax.rem(where_core + dc, 2)
        )

    barrier = pltpu.get_barrier_semaphore()
    for k in range(1, seq_count):
        pl.semaphore_signal(barrier, inc=1, device_id=(kv_me, at(k)), device_id_type=MESH)
    for k in range(1, kv_count):
        pl.semaphore_signal(
            barrier, inc=1, device_id=(lax.rem(kv_me + k, kv_count), me), device_id_type=MESH
        )

    small[5].start()
    small[6].start()

    small[0].wait()
    small[1].wait()
    table_t = table[...]
    for r in range(8):
        query_flat[pl.ds(4 * r, 4), :] = query[r].astype(F32)

    lane = iota((64, 128), 1)
    row = iota((64, 128), 0)
    diag = lane == row
    own_pick = (iota((256, 128), 0) == 8 * me + (iota((256, 128), 1) & 7)).astype(F32).astype(BF16)
    keep_lane = (iota((8, 128), 1) >> 3) == iota((8, 128), 0)

    def own_row(x):
        y = dot(x.astype(F32).astype(BF16), own_pick)
        return jnp.sum(jnp.where(keep_lane, y, 0.0), axis=0, keepdims=True)

    inside = iota((1, 128), 1) < 64
    holder_row = jnp.where(inside, own_row(table_t >> 6), -1.0)
    page_row = holder_row * 64.0 + own_row(table_t & 63)

    def to_col(x):
        return jnp.sum(jnp.where(diag, x, 0.0), axis=1, keepdims=True)

    earlier = jnp.logical_and(to_col(holder_row) == holder_row, to_col(page_row) < page_row)
    within_row = jnp.sum(earlier.astype(F32), axis=0, keepdims=True)
    entry_row = jnp.where(inside, 2.0 * holder_row + within_row, -1.0)
    slot_of = (2 * (row & 31) + (row >> 5)).astype(F32)
    entry_pick = (entry_row == slot_of).astype(F32)
    entry_pick_b = entry_pick.astype(BF16)
    picked = dot(
        entry_pick_b,
        jnp.concatenate(
            [jnp.concatenate([query_flat[pl.ds(h, 8, stride=4), :]] * 16, axis=0) for h in range(4)],
            axis=1,
        ).astype(BF16),
    )
    for k in range(2):
        for h in range(4):
            query_send.reshape(256, 128)[pl.ds(k * 4 + h, 32, stride=8), :] = picked[
                k * 32 : k * 32 + 32, h * 128 : h * 128 + 128
            ]
    def query_copy(k):
        other = at(k)
        return pltpu.make_async_remote_copy(
            src_ref=query_send.at[other],
            dst_ref=query_recv.at[me],
            send_sem=query_send_sem,
            recv_sem=query_recv_sems.at[me],
            device_id=(kv_me, other),
            device_id_type=MESH,
        )

    pl.semaphore_wait(barrier, seq_count - 1 + kv_count - 1)
    for k in range(1, seq_count):
        query_copy(k).start()
    query_recv[me] = query_send[me]

    request_col = jnp.sum(entry_pick * (lane & 7).astype(F32), axis=1, keepdims=True)
    request_is = ((iota((8, 128), 1) & 7) == iota((8, 128), 0)).astype(F32).astype(BF16)
    gather = dot_nt(request_is, entry_pick_b)

    small[2].wait()
    valid_count, owner = place_pages(table_t, lengths, me)
    owner_col = owner.astype(F32)
    owner_row = jnp.where(inside, to_row(owner_col, diag), -1.0)
    before = jnp.logical_and(owner_col == owner_row, lane < row)
    slot_col = 2.0 * owner_col + jnp.sum(before.astype(F32), axis=1, keepdims=True)
    order_row = jnp.where(slot_col == lane.astype(F32), row.astype(F32), 0.0)
    order_vmem[...] = jnp.sum(order_row, axis=0, keepdims=True).astype(I32)
    order_copy = pltpu.make_async_copy(order_vmem, order, order_sem)
    order_copy.start()

    small[3].wait()
    small[4].wait()
    rows = (target_rows, count_rows, divisor_rows, fold_rows)
    mass = plan_pages(valid_count, keep, weight, rows)
    mass_ref[...] = mass
    mass_rows[...] = mass.astype(F32)

    @pl.loop(0, 64 // CHUNK)
    def _(i):
        page_copy(i).wait()
        for j in range(CHUNK):
            compact_page(i * CHUNK + j, pages, packed_ref, rows)

    small[5].wait()
    for r in range(8):
        for c in range(2):
            both = fresh[r, c].astype(F32)
            for g in range(2):
                fresh_flat[pl.ds((c * 2 + g) * 8 + r, 1), :] = both[g : g + 1, :]
    score_scale = 128 ** -0.5
    lane8 = iota((8, 128), 1)
    row8 = iota((8, 128), 0)
    own = jnp.zeros((8, 128), F32)
    for h in range(4):
        q = query_flat[pl.ds(h, 8, stride=4), :]
        key = fresh_flat[pl.ds((h // 2) * 8, 8), :]
        own = jnp.where(lane8 == h, jnp.sum(q * key, axis=1, keepdims=True) * score_scale, own)

    order_copy.wait()
    first = row8 < 4
    head_low = (row8 & 3) < 2

    def pages_of(o):
        return order[0, 2 * o] & 63, order[0, 2 * o + 1] & 63

    def scores(k):
        o = at(k)
        a, b = pages_of(o)
        q = query_recv[o]
        q = jnp.concatenate(
            [jnp.where(head_low, q, 0.0), jnp.where(head_low, 0.0, q)], axis=1
        ).astype(BF16)
        keys = [jnp.concatenate([packed_ref[p, 0, 0], packed_ref[p, 0, 1]], axis=1) for p in (a, b)]
        score_rows[k - 1] = jnp.where(first, dot_nt(q, keys[0]), dot_nt(q, keys[1])) * score_scale

    def finish(k):
        o = at(k)
        a, b = pages_of(o)
        page_mass = jnp.where(first, mass_rows[pl.ds(a, 1), :], mass_rows[pl.ds(b, 1), :])
        live = page_mass > 0.0
        score = score_rows[k - 1]
        top = jnp.max(jnp.where(live, score, floor_value), axis=1, keepdims=True)
        w = jnp.where(live, page_mass * jnp.exp(score - top), 0.0)
        total = jnp.sum(w, axis=1, keepdims=True)
        w = w.astype(BF16)
        values = [jnp.concatenate([packed_ref[p, 1, 0], packed_ref[p, 1, 1]], axis=1) for p in (a, b)]
        part = jnp.where(jnp.concatenate([first, first], axis=1), dot(w, values[0]), dot(w, values[1]))
        part_send[o, pl.ds(0, 8), :] = jnp.where(head_low, part[:, :128], part[:, 128:])
        stat = jnp.where(lane8 == row8, top, jnp.where(lane8 == row8 + 8, total, 0.0))
        part_send[o, pl.ds(8, 1), :] = jnp.sum(stat, axis=0, keepdims=True)

    def part_copy(k):
        other = at(k)
        return pltpu.make_async_remote_copy(
            src_ref=part_send.at[other, pl.ds(0, 9)],
            dst_ref=part_recv.at[me, pl.ds(0, 9)],
            send_sem=part_sems.at[0],
            recv_sem=part_sems.at[1],
            device_id=(kv_me, other),
            device_id_type=MESH,
        )

    def query_wait(k):
        o = at(k)
        pltpu.make_async_remote_copy(
            src_ref=query_send.at[o],
            dst_ref=query_recv.at[o],
            send_sem=query_send_sem,
            recv_sem=query_recv_sems.at[o],
            device_id=(kv_me, o),
            device_id_type=MESH,
        ).wait_recv()

    def group(i):
        return [GROUP * i + j + 1 for j in range(GROUP)]

    for i in range(seq_count // GROUP):
        others = [k for k in group(i) if k < seq_count]
        for k in others:
            query_wait(k)
        for k in group(i):
            scores(k)
        if i > 0:
            for k in group(i - 1):
                finish(k)
            for k in group(i - 1):
                part_copy(k).start()
    for k in group(i):
        finish(k)
    for k in others:
        part_copy(k).start()
    part_recv[me] = part_send[me]

    def all_of(send, recv, send_sem, recv_sem, n, *rest):
        return pltpu.make_async_remote_copy(
            src_ref=send.at[(pl.ds(0, n), *rest)],
            dst_ref=recv.at[(pl.ds(0, n), *rest)],
            send_sem=send_sem,
            recv_sem=recv_sem,
            device_id=(kv_me, me),
            device_id_type=MESH,
        )

    all_parts = all_of(
        part_send, part_recv, part_sems.at[0], part_sems.at[1], seq_count - 1, pl.ds(0, 9)
    )
    all_parts.wait_recv()
    part_recv_flat = part_recv.reshape(512, 128)
    stats = part_recv_flat[pl.ds(8, 32, stride=16), :]
    top = jnp.concatenate([stats, pltpu.roll(stats, 124, 1)], axis=0)
    total = jnp.concatenate([pltpu.roll(stats, 120, 1), pltpu.roll(stats, 116, 1)], axis=0)
    top = jnp.where(lane < 4, top, 0.0)
    total = jnp.where(lane < 4, total, 0.0)
    best = own
    for r in range(8):
        one = jnp.max(jnp.where(request_col == float(r), top, floor_value), axis=0, keepdims=True)
        best = jnp.where(jnp.logical_and(row8 == r, lane8 < 4), jnp.maximum(best, one), best)
    best_rows = jnp.zeros((64, 128), F32)
    for r in range(8):
        best_rows = jnp.where(request_col == float(r), best[r : r + 1, :], best_rows)
    factor = jnp.exp(top - best_rows)
    scaled = [
        factor[:, h : h + 1]
        * jnp.concatenate(
            [part_recv_flat[pl.ds(k * 4 + h, 32, stride=16), :] for k in range(2)], axis=0
        )
        for h in range(4)
    ]
    gather_b = gather.astype(BF16)
    sums = sum(
        dot(gather_b, piece) for piece in split(jnp.concatenate(scaled + [factor * total], axis=1), 3)
    )
    own_factor = jnp.exp(own - best)
    denominator = sums[:, 512:] + own_factor
    attended = jnp.concatenate(
        [
            (
                sums[:, h * 128 : h * 128 + 128]
                + own_factor[:, h : h + 1] * fresh_flat[pl.ds(16 + (h // 2) * 8, 8), :]
            )
            / denominator[:, h : h + 1]
            for h in range(4)
        ],
        axis=1,
    ).astype(BF16)
    attended_ref[...] = attended

    small[6].wait()

    def sum_block(k):
        other = lax.rem(kv_me + k, kv_count)
        return dot(attended, out_weight[:, pl.ds(pl.multiple_of(other * 512, 512), 512)])

    for k in (2, 1, 3):
        other = lax.rem(kv_me + k, kv_count)
        sum_send[other] = sum_block(k).astype(BF16)
        pltpu.make_async_remote_copy(
            src_ref=sum_send.at[other],
            dst_ref=sum_recv.at[k - 1],
            send_sem=sum_sems.at[0],
            recv_sem=sum_sems.at[1],
            device_id=(other, me),
            device_id_type=MESH,
        ).start()
    mine = sum_block(0)
    all_parts.wait_send()
    all_of(query_send, query_recv, query_send_sem, query_recv_sems.at[0], seq_count - 1).wait_send()
    all_sums = all_of(sum_send, sum_recv, sum_sems.at[0], sum_sems.at[1], kv_count - 1)
    all_sums.wait_recv()
    for k in range(3):
        mine = mine + sum_recv[k].astype(F32)
    projected_ref[...] = mine.astype(BF16)
    all_sums.wait_send()


def early_kernel(
    page_hbm, keep_hbm, weight_hbm, table_hbm, lengths_hbm, out_hbm,
    pages, packed, keep, weight, table, lengths,
    target_rows, count_rows, fold_rows, divisor_rows, page_sem, in_sem, out_sem,
):
    me = lax.axis_index("seq")
    pieces = share()

    def page_copy(i):
        at = pl.ds(i * 8, 8)
        return pltpu.make_async_copy(page_hbm.at[at], pages.at[at], page_sem.at[i])

    def out_copy(i):
        at = pl.ds(i * 8, 8)
        return pltpu.make_async_copy(packed.at[at], out_hbm.at[at], out_sem.at[i])

    @pl.when(pieces > 0)
    def _():
        small = [
            pltpu.make_async_copy(src, dst, in_sem.at[i])
            for i, (src, dst) in enumerate(
                [(table_hbm, table), (lengths_hbm, lengths), (keep_hbm, keep), (weight_hbm, weight)]
            )
        ]
        for copy in small:
            copy.start()
        pl.loop(0, pieces)(lambda i: page_copy(i).start())
        for copy in small:
            copy.wait()
        valid_count, _ = place_pages(table[...], lengths, me)
        rows = (target_rows, count_rows, divisor_rows, fold_rows)
        plan_pages(valid_count, keep, weight, rows)

        @pl.loop(0, pieces)
        def _(i):
            page_copy(i).wait()
            for j in range(8):
                compact_page(i * 8 + j, pages, packed, rows)
            out_copy(i).start()

        pl.loop(0, pieces)(lambda i: out_copy(i).wait())


def write_kernel(packed, mass, attended, projected, early, *rest):
    outs, sems = rest[:4], rest[4]
    pieces = share()

    def packed_copy(i):
        at = pl.ds(i * 8, 8)
        return pltpu.make_async_copy(packed.at[at], outs[0].at[at], sems.at[3 + i])

    small = [
        pltpu.make_async_copy(src, dst, sems.at[i])
        for i, (src, dst) in enumerate(zip((mass, attended, projected), outs[1:]))
    ]
    pl.loop(pieces, 8)(lambda i: packed_copy(i).start())
    for copy in small:
        copy.start()
    for copy in small:
        copy.wait()
    pl.loop(pieces, 8)(lambda i: packed_copy(i).wait())


def per_device(
    page_cache, keep_list, fold_weight, page_table, lengths, queries, fresh_entries, out_weight
):
    anywhere = pl.BlockSpec(memory_space=pl.ANY)
    shapes = [((64, 2, 2, 128, 128), BF16), ((64, 128), BF16), ((8, 512), BF16), ((8, 512), BF16)]
    page_cache, keep_list, fold_weight, table_t, lengths, queries, fresh_entries, out_weight = (
        pltpu.with_memory_space_constraint(x, pltpu.HBM)
        for x in (
            page_cache, keep_list, fold_weight, page_table.T, lengths.reshape(2, 128), queries,
            fresh_entries, out_weight,
        )
    )
    early = pl.pallas_call(
        early_kernel,
        out_shape=pltpu.HBM(*shapes[0]),
        in_specs=[anywhere] * 5,
        out_specs=anywhere,
        scratch_shapes=[
            pltpu.VMEM((64, 2, 2, 128, 128), BF16),
            pltpu.VMEM((64, 2, 2, 128, 128), BF16),
            pltpu.VMEM((64, 128), I32),
            pltpu.VMEM((64, 128), F32),
            pltpu.VMEM((8, 256), I32),
            pltpu.VMEM((2, 128), I32),
            pltpu.VMEM((64, 128), F32),
            pltpu.VMEM((64, 128), F32),
            pltpu.VMEM((3, 64, 128), F32),
            pltpu.VMEM((64, 128), F32),
            pltpu.SemaphoreType.DMA((8,)),
            pltpu.SemaphoreType.DMA((4,)),
            pltpu.SemaphoreType.DMA((8,)),
        ],
        compiler_params=pltpu.CompilerParams(has_side_effects=True, vmem_limit_bytes=36 << 20),
        name="early",
    )(page_cache, keep_list, fold_weight, table_t, lengths)
    results = pl.pallas_call(
        main_kernel,
        out_shape=[pltpu.VMEM(shape, dtype) for shape, dtype in shapes],
        in_specs=[anywhere] * 9,
        out_specs=[pl.BlockSpec(memory_space=pltpu.VMEM)] * 4,
        scratch_shapes=[
            pltpu.VMEM((64, 2, 2, 128, 128), BF16),
            pltpu.VMEM((64, 128), I32),
            pltpu.VMEM((64, 128), F32),
            pltpu.VMEM((8, 256), I32),
            pltpu.VMEM((2, 128), I32),
            pltpu.VMEM((8, 4, 128), BF16),
            pltpu.VMEM((8, 2, 2, 128), BF16),
            pltpu.VMEM((512, 2048), BF16),
            pltpu.VMEM((32, 128), F32),
            pltpu.VMEM((32, 128), F32),
            pltpu.VMEM((32, 8, 128), F32),
            pltpu.VMEM((32, 8, 128), F32),
            pltpu.VMEM((32, 16, 128), F32),
            pltpu.VMEM((32, 16, 128), F32),
            pltpu.VMEM((4, 8, 512), BF16),
            pltpu.VMEM((4, 8, 512), BF16),
            pltpu.VMEM((64, 128), F32),
            pltpu.VMEM((64, 128), F32),
            pltpu.VMEM((3, 64, 128), F32),
            pltpu.VMEM((64, 128), F32),
            pltpu.VMEM((64, 128), F32),
            pltpu.VMEM((32, 8, 128), F32),
            pltpu.VMEM((1, 128), I32),
            pltpu.SMEM((1, 128), I32),
            pltpu.SemaphoreType.DMA((64 // CHUNK,)),
            pltpu.SemaphoreType.DMA((7,)),
            pltpu.SemaphoreType.DMA,
            pltpu.SemaphoreType.DMA((32,)),
            pltpu.SemaphoreType.DMA((2,)),
            pltpu.SemaphoreType.DMA((2,)),
            pltpu.SemaphoreType.DMA,
        ],
        compiler_params=pltpu.CompilerParams(
            collective_id=0, has_side_effects=True, vmem_limit_bytes=36 << 20
        ),
        name="decode",
    )(
        page_cache, keep_list, fold_weight, table_t, lengths, queries, fresh_entries, out_weight,
        pltpu.with_memory_space_constraint(early, pltpu.HBM),
    )
    return tuple(
        pl.pallas_call(
            write_kernel,
            out_shape=[pltpu.HBM(shape, dtype) for shape, dtype in shapes],
            in_specs=[anywhere] * 5,
            out_specs=[anywhere] * 4,
            scratch_shapes=[pltpu.SemaphoreType.DMA((11,))],
            input_output_aliases={4: 0},
            compiler_params=pltpu.CompilerParams(vmem_limit_bytes=1 << 20),
            name="write",
        )(*results, early)
    )


def solution(mesh):
    placed = (
        P("seq", None, "kv", None, None),
        P("seq", None),
        P("seq", None),
        P(),
        P(),
        P("seq", "kv", None),
        P("seq", None, "kv", None),
        P("kv", None),
    )
    return jax.shard_map(
        per_device,
        mesh=mesh,
        in_specs=placed,
        out_specs=(
            P("seq", None, "kv", None, None),
            P("seq", None),
            P("seq", "kv"),
            P("seq", "kv"),
        ),
        check_vma=False,
    )
```

```python
import functools

import jax
import jax.numpy as jnp
from jax import lax
from jax.experimental import pallas as pl
from jax.experimental.pallas import tpu as pltpu
from jax.sharding import PartitionSpec as P

MESH = pl.DeviceIdType.MESH
F32 = jnp.float32
BF16 = jnp.bfloat16
I32 = jnp.int32
floor_value = -1e30
CHUNK = 16
LEAD = 28
GROUP = 8
PEERS = sorted(
    ((dz, dx, dc) for dz in range(4) for dx in range(4) for dc in range(2)),
    key=lambda d: (-min(d[0], 4 - d[0]) - min(d[1], 4 - d[1]), -d[2], d),
)


def iota(shape, axis):
    return lax.broadcasted_iota(I32, shape, axis)


def split(x, parts):
    out = []
    for _ in range(parts):
        piece = x.astype(BF16)
        out.append(piece)
        x = x - piece.astype(F32)
    return out


def dot(a, b):
    return jnp.dot(a, b, preferred_element_type=F32)


def dot_nt(a, b):
    return lax.dot_general(a, b, (((1,), (1,)), ((), ())), preferred_element_type=F32)


def one_hot_dot(mask, x, parts):
    sel = mask.astype(F32).astype(BF16)
    return sum(dot(sel, piece) for piece in split(x, parts))


def to_row(col, diag):
    return jnp.sum(jnp.where(diag, col, 0.0), axis=0, keepdims=True)


def place_pages(table_t, lengths, me):
    lengths_row = jnp.concatenate([lengths[0:1, :], lengths[1:2, :]], axis=1)
    number = iota((8, 256), 0)
    request = iota((8, 256), 1)
    codes = (jnp.clip(lengths_row - 128 * number, 0, 128) + 256 * (request >> 3)).astype(F32)
    here = iota((64, 256), 0) + 64 * me
    code = jnp.zeros((64, 256), F32)
    for j in range(8):
        code = code + jnp.where(table_t[j : j + 1, :] == here, codes[j : j + 1, :], 0.0)
    code = jnp.sum(code, axis=1, keepdims=True).astype(I32)
    return code & 255, code >> 8


def plan_pages(valid_count, keep, weight, rows):
    target_rows, count_rows, divisor_rows, fold_rows = rows
    lane = iota((64, 128), 1)
    valid = lane < valid_count
    kept = jnp.logical_and(valid, keep[...] > 0)
    dropped = jnp.logical_and(valid, keep[...] == 0)
    kept_flag = kept.astype(F32)
    upper = (iota((128, 128), 0) < iota((128, 128), 1)).astype(F32).astype(BF16)
    position = dot(kept_flag.astype(BF16), upper)
    count = jnp.sum(kept_flag, axis=1, keepdims=True)
    dropped_weight = jnp.where(dropped, weight[...], 0.0)
    weight_sum = jnp.sum(dropped_weight, axis=1, keepdims=True)
    target_rows[...] = jnp.where(kept, position, -1.0)
    count_rows[...] = jnp.broadcast_to(count, (64, 128))
    divisor_rows[...] = jnp.broadcast_to(jnp.maximum(weight_sum, 1.0), (64, 128))
    for i, piece in enumerate(split(dropped_weight, 3)):
        fold_rows[i] = piece.astype(F32)
    lane_f = lane.astype(F32)
    mass = jnp.where(lane_f < count, 1.0, jnp.where(lane_f == count, weight_sum, 0.0)).astype(BF16)
    return mass


def compact_page(p, pages, packed_ref, rows):
    target_rows, count_rows, divisor_rows, fold_rows = rows
    slots = iota((128, 128), 0).astype(F32)
    extra_row = iota((16, 128), 0)
    target = target_rows[pl.ds(p, 1), :]
    picks = jnp.where(slots == target, 1.0, 0.0)
    extra = jnp.where(extra_row == 0, fold_rows[0, pl.ds(p, 1), :], 0.0)
    extra = jnp.where(extra_row == 1, fold_rows[1, pl.ds(p, 1), :], extra)
    extra = jnp.where(extra_row == 2, fold_rows[2, pl.ds(p, 1), :], extra)
    lhs = jnp.concatenate([picks.astype(BF16), extra.astype(BF16)], axis=0)
    page = jnp.concatenate(
        [pages[p, 0, 0], pages[p, 0, 1], pages[p, 1, 0], pages[p, 1, 1]], axis=1
    )
    moved = dot(lhs, page)
    divisor = divisor_rows[pl.ds(p, 1), :]
    folded = jnp.sum(moved[128:136, :], axis=0, keepdims=True)
    at_fold = slots == count_rows[pl.ds(p, 1), :]
    for i in range(4):
        cols = slice(128 * i, 128 * i + 128)
        packed_ref[p, i // 2, i % 2] = jnp.where(
            at_fold, folded[:, cols] / divisor, moved[:128, cols]
        ).astype(BF16)


def share():
    kv_me, me = lax.axis_index("kv"), lax.axis_index("seq")

    def pick(i, values):
        out = values[-1]
        for at in range(len(values) - 1):
            out = jnp.where(i == at, values[at], out)
        return out

    lead = (
        pick(kv_me, (0, 11, 18, 21))
        + pick(me // 8, (0, 13, 27, 29))
        + pick(lax.rem(me // 2, 4), (0, 9, 13, 12))
        + 8 * lax.rem(me, 2)
    )
    return jnp.clip((LEAD - lead + 3) // 4, 0, 8)


def main_kernel(
    page_hbm, keep_hbm, weight_hbm, table_hbm, lengths_hbm, query_hbm, fresh_hbm, out_weight_hbm,
    early,
    packed_ref, mass_ref, attended_ref, projected_ref,
    pages, keep, weight, table, lengths, query, fresh, out_weight,
    query_flat, fresh_flat, query_tiles, query_send, query_recv, part_send, part_recv, sum_send, sum_recv,
    target_rows, count_rows, fold_rows, divisor_rows, mass_rows, score_rows, order_vmem, order,
    page_sem, in_sem, query_send_sem, query_recv_sems, part_sems, sum_sems, order_sem,
):
    kv_count, seq_count = lax.axis_size("kv"), lax.axis_size("seq")
    kv_me, me = lax.axis_index("kv"), lax.axis_index("seq")

    def page_copy(i):
        return pltpu.make_async_copy(
            page_hbm.at[pl.ds(i * CHUNK, CHUNK)], pages.at[pl.ds(i * CHUNK, CHUNK)], page_sem.at[i]
        )

    small = [
        pltpu.make_async_copy(src, dst, in_sem.at[i])
        for i, (src, dst) in enumerate(
            [(table_hbm, table), (query_hbm, query), (lengths_hbm, lengths), (keep_hbm, keep),
             (weight_hbm, weight), (fresh_hbm, fresh), (out_weight_hbm, out_weight)]
        )
    ]
    for copy in small[:5]:
        copy.start()

    @pl.loop(0, 64 // CHUNK)
    def _(i):
        page_copy(i).start()

    where_z, where_x, where_core = me // 8, lax.rem(me // 2, 4), lax.rem(me, 2)

    def at(k):
        dz, dx, dc = PEERS[k - 1]
        return (
            lax.rem(where_z + dz, 4) * 8 + lax.rem(where_x + dx, 4) * 2 + lax.rem(where_core + dc, 2)
        )

    barrier = pltpu.get_barrier_semaphore()
    for k in range(1, seq_count):
        pl.semaphore_signal(barrier, inc=1, device_id=(kv_me, at(k)), device_id_type=MESH)
    for k in range(1, kv_count):
        pl.semaphore_signal(
            barrier, inc=1, device_id=(lax.rem(kv_me + k, kv_count), me), device_id_type=MESH
        )

    small[5].start()
    small[6].start()

    small[0].wait()
    small[1].wait()
    table_t = table[...]
    for r in range(8):
        query_flat[pl.ds(4 * r, 4), :] = query[r].astype(F32)

    lane = iota((64, 128), 1)
    row = iota((64, 128), 0)
    diag = lane == row
    own_pick = (iota((256, 128), 0) == 8 * me + (iota((256, 128), 1) & 7)).astype(F32).astype(BF16)
    keep_lane = (iota((8, 128), 1) >> 3) == iota((8, 128), 0)

    def own_row(x):
        y = dot(x.astype(F32).astype(BF16), own_pick)
        return jnp.sum(jnp.where(keep_lane, y, 0.0), axis=0, keepdims=True)

    inside = iota((1, 128), 1) < 64
    holder_row = jnp.where(inside, own_row(table_t >> 6), -1.0)
    page_row = holder_row * 64.0 + own_row(table_t & 63)

    def to_col(x):
        return jnp.sum(jnp.where(diag, x, 0.0), axis=1, keepdims=True)

    earlier = jnp.logical_and(to_col(holder_row) == holder_row, to_col(page_row) < page_row)
    within_row = jnp.sum(earlier.astype(F32), axis=0, keepdims=True)
    entry_row = jnp.where(inside, 2.0 * holder_row + within_row, -1.0)
    slot_of = (2 * (row & 31) + (row >> 5)).astype(F32)
    entry_pick = (entry_row == slot_of).astype(F32)
    entry_pick_b = entry_pick.astype(BF16)
    picked = dot(
        entry_pick_b,
        jnp.concatenate(
            [jnp.concatenate([query_flat[pl.ds(h, 8, stride=4), :]] * 16, axis=0) for h in range(4)],
            axis=1,
        ).astype(BF16),
    )
    for k in range(2):
        for h in range(4):
            query_tiles.reshape(256, 128)[pl.ds(k * 4 + h, 32, stride=8), :] = picked[
                k * 32 : k * 32 + 32, h * 128 : h * 128 + 128
            ]
    query_send[...] = query_tiles[...].astype(BF16)
    def query_copy(k):
        other = at(k)
        return pltpu.make_async_remote_copy(
            src_ref=query_send.at[other],
            dst_ref=query_recv.at[me],
            send_sem=query_send_sem,
            recv_sem=query_recv_sems.at[me],
            device_id=(kv_me, other),
            device_id_type=MESH,
        )


    request_col = jnp.sum(entry_pick * (lane & 7).astype(F32), axis=1, keepdims=True)
    request_is = ((iota((8, 128), 1) & 7) == iota((8, 128), 0)).astype(F32).astype(BF16)
    gather = dot_nt(request_is, entry_pick_b)

    small[2].wait()
    valid_count, owner = place_pages(table_t, lengths, me)
    owner_col = owner.astype(F32)
    owner_row = jnp.where(inside, to_row(owner_col, diag), -1.0)
    before = jnp.logical_and(owner_col == owner_row, lane < row)
    slot_col = 2.0 * owner_col + jnp.sum(before.astype(F32), axis=1, keepdims=True)
    order_row = jnp.where(slot_col == lane.astype(F32), row.astype(F32), 0.0)
    order_vmem[...] = jnp.sum(order_row, axis=0, keepdims=True).astype(I32)
    order_copy = pltpu.make_async_copy(order_vmem, order, order_sem)
    order_copy.start()

    small[3].wait()
    small[4].wait()
    rows = (target_rows, count_rows, divisor_rows, fold_rows)
    mass = plan_pages(valid_count, keep, weight, rows)
    mass_ref[...] = mass
    mass_rows[...] = mass.astype(F32)

    pl.semaphore_wait(barrier, seq_count - 1 + kv_count - 1)
    for k in range(1, seq_count):
        query_copy(k).start()
    query_recv[me] = query_send[me]

    @pl.loop(0, 64 // CHUNK)
    def _(i):
        page_copy(i).wait()
        for j in range(CHUNK):
            compact_page(i * CHUNK + j, pages, packed_ref, rows)

    small[5].wait()
    for r in range(8):
        for c in range(2):
            both = fresh[r, c].astype(F32)
            for g in range(2):
                fresh_flat[pl.ds((c * 2 + g) * 8 + r, 1), :] = both[g : g + 1, :]
    score_scale = 128 ** -0.5
    lane8 = iota((8, 128), 1)
    row8 = iota((8, 128), 0)
    own = jnp.zeros((8, 128), F32)
    for h in range(4):
        q = query_flat[pl.ds(h, 8, stride=4), :]
        key = fresh_flat[pl.ds((h // 2) * 8, 8), :]
        own = jnp.where(lane8 == h, jnp.sum(q * key, axis=1, keepdims=True) * score_scale, own)

    order_copy.wait()
    first = row8 < 4
    head_low = (row8 & 3) < 2

    def pages_of(o):
        return order[0, 2 * o] & 63, order[0, 2 * o + 1] & 63

    def scores(k):
        o = at(k)
        a, b = pages_of(o)
        q = query_recv[o].astype(F32)
        q = jnp.concatenate(
            [jnp.where(head_low, q, 0.0), jnp.where(head_low, 0.0, q)], axis=1
        ).astype(BF16)
        keys = [jnp.concatenate([packed_ref[p, 0, 0], packed_ref[p, 0, 1]], axis=1) for p in (a, b)]
        score_rows[k - 1] = jnp.where(first, dot_nt(q, keys[0]), dot_nt(q, keys[1])) * score_scale

    def finish(k):
        o = at(k)
        a, b = pages_of(o)
        page_mass = jnp.where(first, mass_rows[pl.ds(a, 1), :], mass_rows[pl.ds(b, 1), :])
        live = page_mass > 0.0
        score = score_rows[k - 1]
        top = jnp.max(jnp.where(live, score, floor_value), axis=1, keepdims=True)
        w = jnp.where(live, page_mass * jnp.exp(score - top), 0.0)
        total = jnp.sum(w, axis=1, keepdims=True)
        w = w.astype(BF16)
        values = [jnp.concatenate([packed_ref[p, 1, 0], packed_ref[p, 1, 1]], axis=1) for p in (a, b)]
        part = jnp.where(jnp.concatenate([first, first], axis=1), dot(w, values[0]), dot(w, values[1]))
        part_send[o, pl.ds(0, 8), :] = jnp.where(head_low, part[:, :128], part[:, 128:])
        stat = jnp.where(lane8 == row8, top, jnp.where(lane8 == row8 + 8, total, 0.0))
        part_send[o, pl.ds(8, 1), :] = jnp.sum(stat, axis=0, keepdims=True)

    def part_copy(k):
        other = at(k)
        return pltpu.make_async_remote_copy(
            src_ref=part_send.at[other, pl.ds(0, 9)],
            dst_ref=part_recv.at[me, pl.ds(0, 9)],
            send_sem=part_sems.at[0],
            recv_sem=part_sems.at[1],
            device_id=(kv_me, other),
            device_id_type=MESH,
        )

    def query_wait(k):
        o = at(k)
        pltpu.make_async_remote_copy(
            src_ref=query_send.at[o],
            dst_ref=query_recv.at[o],
            send_sem=query_send_sem,
            recv_sem=query_recv_sems.at[o],
            device_id=(kv_me, o),
            device_id_type=MESH,
        ).wait_recv()

    def group(i):
        return [GROUP * i + j + 1 for j in range(GROUP)]

    for i in range(seq_count // GROUP):
        others = [k for k in group(i) if k < seq_count]
        for k in others:
            query_wait(k)
        for k in group(i):
            scores(k)
        if i > 0:
            for k in group(i - 1):
                finish(k)
            for k in group(i - 1):
                part_copy(k).start()
    for k in group(i):
        finish(k)
    for k in others:
        part_copy(k).start()
    part_recv[me] = part_send[me]

    def all_of(send, recv, send_sem, recv_sem, n, *rest):
        return pltpu.make_async_remote_copy(
            src_ref=send.at[(pl.ds(0, n), *rest)],
            dst_ref=recv.at[(pl.ds(0, n), *rest)],
            send_sem=send_sem,
            recv_sem=recv_sem,
            device_id=(kv_me, me),
            device_id_type=MESH,
        )

    all_parts = all_of(
        part_send, part_recv, part_sems.at[0], part_sems.at[1], seq_count - 1, pl.ds(0, 9)
    )
    all_parts.wait_recv()
    part_recv_flat = part_recv.reshape(512, 128)
    stats = part_recv_flat[pl.ds(8, 32, stride=16), :]
    top = jnp.concatenate([stats, pltpu.roll(stats, 124, 1)], axis=0)
    total = jnp.concatenate([pltpu.roll(stats, 120, 1), pltpu.roll(stats, 116, 1)], axis=0)
    top = jnp.where(lane < 4, top, 0.0)
    total = jnp.where(lane < 4, total, 0.0)
    best = own
    for r in range(8):
        one = jnp.max(jnp.where(request_col == float(r), top, floor_value), axis=0, keepdims=True)
        best = jnp.where(jnp.logical_and(row8 == r, lane8 < 4), jnp.maximum(best, one), best)
    best_rows = jnp.zeros((64, 128), F32)
    for r in range(8):
        best_rows = jnp.where(request_col == float(r), best[r : r + 1, :], best_rows)
    factor = jnp.exp(top - best_rows)
    scaled = [
        factor[:, h : h + 1]
        * jnp.concatenate(
            [part_recv_flat[pl.ds(k * 4 + h, 32, stride=16), :] for k in range(2)], axis=0
        )
        for h in range(4)
    ]
    gather_b = gather.astype(BF16)
    sums = sum(
        dot(gather_b, piece) for piece in split(jnp.concatenate(scaled + [factor * total], axis=1), 3)
    )
    own_factor = jnp.exp(own - best)
    denominator = sums[:, 512:] + own_factor
    attended = jnp.concatenate(
        [
            (
                sums[:, h * 128 : h * 128 + 128]
                + own_factor[:, h : h + 1] * fresh_flat[pl.ds(16 + (h // 2) * 8, 8), :]
            )
            / denominator[:, h : h + 1]
            for h in range(4)
        ],
        axis=1,
    ).astype(BF16)
    attended_ref[...] = attended

    small[6].wait()

    def sum_block(k):
        other = lax.rem(kv_me + k, kv_count)
        return dot(attended, out_weight[:, pl.ds(pl.multiple_of(other * 512, 512), 512)])

    for k in (2, 1, 3):
        other = lax.rem(kv_me + k, kv_count)
        sum_send[other] = sum_block(k).astype(BF16)
        pltpu.make_async_remote_copy(
            src_ref=sum_send.at[other],
            dst_ref=sum_recv.at[k - 1],
            send_sem=sum_sems.at[0],
            recv_sem=sum_sems.at[1],
            device_id=(other, me),
            device_id_type=MESH,
        ).start()
    mine = sum_block(0)
    all_parts.wait_send()
    all_of(query_send, query_recv, query_send_sem, query_recv_sems.at[0], seq_count - 1).wait_send()
    all_sums = all_of(sum_send, sum_recv, sum_sems.at[0], sum_sems.at[1], kv_count - 1)
    all_sums.wait_recv()
    for k in range(3):
        mine = mine + sum_recv[k].astype(F32)
    projected_ref[...] = mine.astype(BF16)
    all_sums.wait_send()


def early_kernel(
    page_hbm, keep_hbm, weight_hbm, table_hbm, lengths_hbm, out_hbm,
    pages, packed, keep, weight, table, lengths,
    target_rows, count_rows, fold_rows, divisor_rows, page_sem, in_sem, out_sem,
):
    me = lax.axis_index("seq")
    pieces = share()

    def page_copy(i):
        at = pl.ds(i * 8, 8)
        return pltpu.make_async_copy(page_hbm.at[at], pages.at[at], page_sem.at[i])

    def out_copy(i):
        at = pl.ds(i * 8, 8)
        return pltpu.make_async_copy(packed.at[at], out_hbm.at[at], out_sem.at[i])

    @pl.when(pieces > 0)
    def _():
        small = [
            pltpu.make_async_copy(src, dst, in_sem.at[i])
            for i, (src, dst) in enumerate(
                [(table_hbm, table), (lengths_hbm, lengths), (keep_hbm, keep), (weight_hbm, weight)]
            )
        ]
        for copy in small:
            copy.start()
        pl.loop(0, pieces)(lambda i: page_copy(i).start())
        for copy in small:
            copy.wait()
        valid_count, _ = place_pages(table[...], lengths, me)
        rows = (target_rows, count_rows, divisor_rows, fold_rows)
        plan_pages(valid_count, keep, weight, rows)

        @pl.loop(0, pieces)
        def _(i):
            page_copy(i).wait()
            for j in range(8):
                compact_page(i * 8 + j, pages, packed, rows)
            out_copy(i).start()

        pl.loop(0, pieces)(lambda i: out_copy(i).wait())


def write_kernel(packed, mass, attended, projected, early, *rest):
    outs, sems = rest[:4], rest[4]
    pieces = share()

    def packed_copy(i):
        at = pl.ds(i * 8, 8)
        return pltpu.make_async_copy(packed.at[at], outs[0].at[at], sems.at[3 + i])

    small = [
        pltpu.make_async_copy(src, dst, sems.at[i])
        for i, (src, dst) in enumerate(zip((mass, attended, projected), outs[1:]))
    ]
    pl.loop(pieces, 8)(lambda i: packed_copy(i).start())
    for copy in small:
        copy.start()
    for copy in small:
        copy.wait()
    pl.loop(pieces, 8)(lambda i: packed_copy(i).wait())


def per_device(
    page_cache, keep_list, fold_weight, page_table, lengths, queries, fresh_entries, out_weight
):
    anywhere = pl.BlockSpec(memory_space=pl.ANY)
    shapes = [((64, 2, 2, 128, 128), BF16), ((64, 128), BF16), ((8, 512), BF16), ((8, 512), BF16)]
    page_cache, keep_list, fold_weight, table_t, lengths, queries, fresh_entries, out_weight = (
        pltpu.with_memory_space_constraint(x, pltpu.HBM)
        for x in (
            page_cache, keep_list, fold_weight, page_table.T, lengths.reshape(2, 128), queries,
            fresh_entries, out_weight,
        )
    )
    early = pl.pallas_call(
        early_kernel,
        out_shape=pltpu.HBM(*shapes[0]),
        in_specs=[anywhere] * 5,
        out_specs=anywhere,
        scratch_shapes=[
            pltpu.VMEM((64, 2, 2, 128, 128), BF16),
            pltpu.VMEM((64, 2, 2, 128, 128), BF16),
            pltpu.VMEM((64, 128), I32),
            pltpu.VMEM((64, 128), F32),
            pltpu.VMEM((8, 256), I32),
            pltpu.VMEM((2, 128), I32),
            pltpu.VMEM((64, 128), F32),
            pltpu.VMEM((64, 128), F32),
            pltpu.VMEM((3, 64, 128), F32),
            pltpu.VMEM((64, 128), F32),
            pltpu.SemaphoreType.DMA((8,)),
            pltpu.SemaphoreType.DMA((4,)),
            pltpu.SemaphoreType.DMA((8,)),
        ],
        compiler_params=pltpu.CompilerParams(has_side_effects=True, vmem_limit_bytes=36 << 20),
        name="early",
    )(page_cache, keep_list, fold_weight, table_t, lengths)
    results = pl.pallas_call(
        main_kernel,
        out_shape=[pltpu.VMEM(shape, dtype) for shape, dtype in shapes],
        in_specs=[anywhere] * 9,
        out_specs=[pl.BlockSpec(memory_space=pltpu.VMEM)] * 4,
        scratch_shapes=[
            pltpu.VMEM((64, 2, 2, 128, 128), BF16),
            pltpu.VMEM((64, 128), I32),
            pltpu.VMEM((64, 128), F32),
            pltpu.VMEM((8, 256), I32),
            pltpu.VMEM((2, 128), I32),
            pltpu.VMEM((8, 4, 128), BF16),
            pltpu.VMEM((8, 2, 2, 128), BF16),
            pltpu.VMEM((512, 2048), BF16),
            pltpu.VMEM((32, 128), F32),
            pltpu.VMEM((32, 128), F32),
            pltpu.VMEM((32, 8, 128), F32),
            pltpu.VMEM((32, 8, 128), BF16),
            pltpu.VMEM((32, 8, 128), BF16),
            pltpu.VMEM((32, 16, 128), F32),
            pltpu.VMEM((32, 16, 128), F32),
            pltpu.VMEM((4, 8, 512), BF16),
            pltpu.VMEM((4, 8, 512), BF16),
            pltpu.VMEM((64, 128), F32),
            pltpu.VMEM((64, 128), F32),
            pltpu.VMEM((3, 64, 128), F32),
            pltpu.VMEM((64, 128), F32),
            pltpu.VMEM((64, 128), F32),
            pltpu.VMEM((32, 8, 128), F32),
            pltpu.VMEM((1, 128), I32),
            pltpu.SMEM((1, 128), I32),
            pltpu.SemaphoreType.DMA((64 // CHUNK,)),
            pltpu.SemaphoreType.DMA((7,)),
            pltpu.SemaphoreType.DMA,
            pltpu.SemaphoreType.DMA((32,)),
            pltpu.SemaphoreType.DMA((2,)),
            pltpu.SemaphoreType.DMA((2,)),
            pltpu.SemaphoreType.DMA,
        ],
        compiler_params=pltpu.CompilerParams(
            collective_id=0, has_side_effects=True, vmem_limit_bytes=36 << 20
        ),
        name="decode",
    )(
        page_cache, keep_list, fold_weight, table_t, lengths, queries, fresh_entries, out_weight,
        pltpu.with_memory_space_constraint(early, pltpu.HBM),
    )
    return tuple(
        pl.pallas_call(
            write_kernel,
            out_shape=[pltpu.HBM(shape, dtype) for shape, dtype in shapes],
            in_specs=[anywhere] * 5,
            out_specs=[anywhere] * 4,
            scratch_shapes=[pltpu.SemaphoreType.DMA((11,))],
            input_output_aliases={4: 0},
            compiler_params=pltpu.CompilerParams(vmem_limit_bytes=1 << 20),
            name="write",
        )(*results, early)
    )


def solution(mesh):
    placed = (
        P("seq", None, "kv", None, None),
        P("seq", None),
        P("seq", None),
        P(),
        P(),
        P("seq", "kv", None),
        P("seq", None, "kv", None),
        P("kv", None),
    )
    return jax.shard_map(
        per_device,
        mesh=mesh,
        in_specs=placed,
        out_specs=(
            P("seq", None, "kv", None, None),
            P("seq", None),
            P("seq", "kv"),
            P("seq", "kv"),
        ),
        check_vma=False,
    )
```

```python
import functools

import jax
import jax.numpy as jnp
from jax import lax
from jax.experimental import pallas as pl
from jax.experimental.pallas import tpu as pltpu
from jax.sharding import PartitionSpec as P

MESH = pl.DeviceIdType.MESH
F32 = jnp.float32
BF16 = jnp.bfloat16
I32 = jnp.int32
floor_value = -1e30
CHUNK = 16
LEAD = 28
GROUP = 4
PEERS = sorted(
    ((dz, dx, dc) for dz in range(4) for dx in range(4) for dc in range(2)),
    key=lambda d: (-min(d[0], 4 - d[0]) - min(d[1], 4 - d[1]), -d[2], d),
)


def iota(shape, axis):
    return lax.broadcasted_iota(I32, shape, axis)


def split(x, parts):
    out = []
    for _ in range(parts):
        piece = x.astype(BF16)
        out.append(piece)
        x = x - piece.astype(F32)
    return out


def dot(a, b):
    return jnp.dot(a, b, preferred_element_type=F32)


def dot_nt(a, b):
    return lax.dot_general(a, b, (((1,), (1,)), ((), ())), preferred_element_type=F32)


def one_hot_dot(mask, x, parts):
    sel = mask.astype(F32).astype(BF16)
    return sum(dot(sel, piece) for piece in split(x, parts))


def to_row(col, diag):
    return jnp.sum(jnp.where(diag, col, 0.0), axis=0, keepdims=True)


def place_pages(table_t, lengths, me):
    lengths_row = jnp.concatenate([lengths[0:1, :], lengths[1:2, :]], axis=1)
    number = iota((8, 256), 0)
    request = iota((8, 256), 1)
    codes = (jnp.clip(lengths_row - 128 * number, 0, 128) + 256 * (request >> 3)).astype(F32)
    here = iota((64, 256), 0) + 64 * me
    code = jnp.zeros((64, 256), F32)
    for j in range(8):
        code = code + jnp.where(table_t[j : j + 1, :] == here, codes[j : j + 1, :], 0.0)
    code = jnp.sum(code, axis=1, keepdims=True).astype(I32)
    return code & 255, code >> 8


def plan_pages(valid_count, keep, weight, rows):
    target_rows, count_rows, divisor_rows, fold_rows = rows
    lane = iota((64, 128), 1)
    valid = lane < valid_count
    kept = jnp.logical_and(valid, keep[...] > 0)
    dropped = jnp.logical_and(valid, keep[...] == 0)
    kept_flag = kept.astype(F32)
    upper = (iota((128, 128), 0) < iota((128, 128), 1)).astype(F32).astype(BF16)
    position = dot(kept_flag.astype(BF16), upper)
    count = jnp.sum(kept_flag, axis=1, keepdims=True)
    dropped_weight = jnp.where(dropped, weight[...], 0.0)
    weight_sum = jnp.sum(dropped_weight, axis=1, keepdims=True)
    target_rows[...] = jnp.where(kept, position, -1.0)
    count_rows[...] = jnp.broadcast_to(count, (64, 128))
    divisor_rows[...] = jnp.broadcast_to(jnp.maximum(weight_sum, 1.0), (64, 128))
    for i, piece in enumerate(split(dropped_weight, 3)):
        fold_rows[i] = piece.astype(F32)
    lane_f = lane.astype(F32)
    mass = jnp.where(lane_f < count, 1.0, jnp.where(lane_f == count, weight_sum, 0.0)).astype(BF16)
    return mass


def compact_page(p, pages, packed_ref, rows):
    target_rows, count_rows, divisor_rows, fold_rows = rows
    slots = iota((128, 128), 0).astype(F32)
    extra_row = iota((16, 128), 0)
    target = target_rows[pl.ds(p, 1), :]
    picks = jnp.where(slots == target, 1.0, 0.0)
    extra = jnp.where(extra_row == 0, fold_rows[0, pl.ds(p, 1), :], 0.0)
    extra = jnp.where(extra_row == 1, fold_rows[1, pl.ds(p, 1), :], extra)
    extra = jnp.where(extra_row == 2, fold_rows[2, pl.ds(p, 1), :], extra)
    lhs = jnp.concatenate([picks.astype(BF16), extra.astype(BF16)], axis=0)
    page = jnp.concatenate(
        [pages[p, 0, 0], pages[p, 0, 1], pages[p, 1, 0], pages[p, 1, 1]], axis=1
    )
    moved = dot(lhs, page)
    divisor = divisor_rows[pl.ds(p, 1), :]
    folded = jnp.sum(moved[128:136, :], axis=0, keepdims=True)
    at_fold = slots == count_rows[pl.ds(p, 1), :]
    for i in range(4):
        cols = slice(128 * i, 128 * i + 128)
        packed_ref[p, i // 2, i % 2] = jnp.where(
            at_fold, folded[:, cols] / divisor, moved[:128, cols]
        ).astype(BF16)


def share():
    kv_me, me = lax.axis_index("kv"), lax.axis_index("seq")

    def pick(i, values):
        out = values[-1]
        for at in range(len(values) - 1):
            out = jnp.where(i == at, values[at], out)
        return out

    lead = (
        pick(kv_me, (0, 11, 18, 21))
        + pick(me // 8, (0, 13, 27, 29))
        + pick(lax.rem(me // 2, 4), (0, 9, 13, 12))
        + 8 * lax.rem(me, 2)
    )
    return jnp.clip((LEAD - lead + 3) // 4, 0, 8)


def main_kernel(
    page_hbm, keep_hbm, weight_hbm, table_hbm, lengths_hbm, query_hbm, fresh_hbm, out_weight_hbm,
    early,
    packed_ref, mass_ref, attended_ref, projected_ref,
    pages, keep, weight, table, lengths, query, fresh, out_weight,
    query_flat, fresh_flat, query_tiles, query_send, query_recv, part_send, part_recv, sum_send, sum_recv,
    target_rows, count_rows, fold_rows, divisor_rows, mass_rows, score_rows, order_vmem, order,
    page_sem, in_sem, query_send_sem, query_recv_sems, part_sems, sum_sems, order_sem,
):
    kv_count, seq_count = lax.axis_size("kv"), lax.axis_size("seq")
    kv_me, me = lax.axis_index("kv"), lax.axis_index("seq")

    def page_copy(i):
        return pltpu.make_async_copy(
            page_hbm.at[pl.ds(i * CHUNK, CHUNK)], pages.at[pl.ds(i * CHUNK, CHUNK)], page_sem.at[i]
        )

    small = [
        pltpu.make_async_copy(src, dst, in_sem.at[i])
        for i, (src, dst) in enumerate(
            [(table_hbm, table), (query_hbm, query), (lengths_hbm, lengths), (keep_hbm, keep),
             (weight_hbm, weight), (fresh_hbm, fresh), (out_weight_hbm, out_weight)]
        )
    ]
    for copy in small[:5]:
        copy.start()

    @pl.loop(0, 64 // CHUNK)
    def _(i):
        page_copy(i).start()

    where_z, where_x, where_core = me // 8, lax.rem(me // 2, 4), lax.rem(me, 2)

    def at(k):
        dz, dx, dc = PEERS[k - 1]
        return (
            lax.rem(where_z + dz, 4) * 8 + lax.rem(where_x + dx, 4) * 2 + lax.rem(where_core + dc, 2)
        )

    barrier = pltpu.get_barrier_semaphore()
    for k in range(1, seq_count):
        pl.semaphore_signal(barrier, inc=1, device_id=(kv_me, at(k)), device_id_type=MESH)
    for k in range(1, kv_count):
        pl.semaphore_signal(
            barrier, inc=1, device_id=(lax.rem(kv_me + k, kv_count), me), device_id_type=MESH
        )

    small[5].start()
    small[6].start()

    small[0].wait()
    small[1].wait()
    table_t = table[...]
    for r in range(8):
        query_flat[pl.ds(4 * r, 4), :] = query[r].astype(F32)

    lane = iota((64, 128), 1)
    row = iota((64, 128), 0)
    diag = lane == row
    own_pick = (iota((256, 128), 0) == 8 * me + (iota((256, 128), 1) & 7)).astype(F32).astype(BF16)
    keep_lane = (iota((8, 128), 1) >> 3) == iota((8, 128), 0)

    def own_row(x):
        y = dot(x.astype(F32).astype(BF16), own_pick)
        return jnp.sum(jnp.where(keep_lane, y, 0.0), axis=0, keepdims=True)

    inside = iota((1, 128), 1) < 64
    holder_row = jnp.where(inside, own_row(table_t >> 6), -1.0)
    page_row = holder_row * 64.0 + own_row(table_t & 63)

    def to_col(x):
        return jnp.sum(jnp.where(diag, x, 0.0), axis=1, keepdims=True)

    earlier = jnp.logical_and(to_col(holder_row) == holder_row, to_col(page_row) < page_row)
    within_row = jnp.sum(earlier.astype(F32), axis=0, keepdims=True)
    entry_row = jnp.where(inside, 2.0 * holder_row + within_row, -1.0)
    slot_of = (2 * (row & 31) + (row >> 5)).astype(F32)
    entry_pick = (entry_row == slot_of).astype(F32)
    entry_pick_b = entry_pick.astype(BF16)
    picked = dot(
        entry_pick_b,
        jnp.concatenate(
            [jnp.concatenate([query_flat[pl.ds(h, 8, stride=4), :]] * 16, axis=0) for h in range(4)],
            axis=1,
        ).astype(BF16),
    )
    for k in range(2):
        for h in range(4):
            query_tiles.reshape(256, 128)[pl.ds(k * 4 + h, 32, stride=8), :] = picked[
                k * 32 : k * 32 + 32, h * 128 : h * 128 + 128
            ]
    query_send[...] = query_tiles[...].astype(BF16)
    def query_copy(k):
        other = at(k)
        return pltpu.make_async_remote_copy(
            src_ref=query_send.at[other],
            dst_ref=query_recv.at[me],
            send_sem=query_send_sem,
            recv_sem=query_recv_sems.at[me],
            device_id=(kv_me, other),
            device_id_type=MESH,
        )


    request_col = jnp.sum(entry_pick * (lane & 7).astype(F32), axis=1, keepdims=True)
    request_is = ((iota((8, 128), 1) & 7) == iota((8, 128), 0)).astype(F32).astype(BF16)
    gather = dot_nt(request_is, entry_pick_b)

    small[2].wait()
    valid_count, owner = place_pages(table_t, lengths, me)
    owner_col = owner.astype(F32)
    owner_row = jnp.where(inside, to_row(owner_col, diag), -1.0)
    before = jnp.logical_and(owner_col == owner_row, lane < row)
    slot_col = 2.0 * owner_col + jnp.sum(before.astype(F32), axis=1, keepdims=True)
    order_row = jnp.where(slot_col == lane.astype(F32), row.astype(F32), 0.0)
    order_vmem[...] = jnp.sum(order_row, axis=0, keepdims=True).astype(I32)
    order_copy = pltpu.make_async_copy(order_vmem, order, order_sem)
    order_copy.start()

    small[3].wait()
    small[4].wait()
    rows = (target_rows, count_rows, divisor_rows, fold_rows)
    mass = plan_pages(valid_count, keep, weight, rows)
    mass_ref[...] = mass
    mass_rows[...] = mass.astype(F32)

    pl.semaphore_wait(barrier, seq_count - 1 + kv_count - 1)
    for k in range(1, seq_count):
        query_copy(k).start()
    query_recv[me] = query_send[me]

    @pl.loop(0, 64 // CHUNK)
    def _(i):
        page_copy(i).wait()
        for j in range(CHUNK):
            compact_page(i * CHUNK + j, pages, packed_ref, rows)

    small[5].wait()
    for r in range(8):
        for c in range(2):
            both = fresh[r, c].astype(F32)
            for g in range(2):
                fresh_flat[pl.ds((c * 2 + g) * 8 + r, 1), :] = both[g : g + 1, :]
    score_scale = 128 ** -0.5
    lane8 = iota((8, 128), 1)
    row8 = iota((8, 128), 0)
    own = jnp.zeros((8, 128), F32)
    for h in range(4):
        q = query_flat[pl.ds(h, 8, stride=4), :]
        key = fresh_flat[pl.ds((h // 2) * 8, 8), :]
        own = jnp.where(lane8 == h, jnp.sum(q * key, axis=1, keepdims=True) * score_scale, own)

    order_copy.wait()
    first = row8 < 4
    head_low = (row8 & 3) < 2

    def pages_of(o):
        return order[0, 2 * o] & 63, order[0, 2 * o + 1] & 63

    def scores(k):
        o = at(k)
        a, b = pages_of(o)
        q = query_recv[o].astype(F32)
        q = jnp.concatenate(
            [jnp.where(head_low, q, 0.0), jnp.where(head_low, 0.0, q)], axis=1
        ).astype(BF16)
        keys = [jnp.concatenate([packed_ref[p, 0, 0], packed_ref[p, 0, 1]], axis=1) for p in (a, b)]
        score_rows[k - 1] = jnp.where(first, dot_nt(q, keys[0]), dot_nt(q, keys[1])) * score_scale

    def finish(k):
        o = at(k)
        a, b = pages_of(o)
        page_mass = jnp.where(first, mass_rows[pl.ds(a, 1), :], mass_rows[pl.ds(b, 1), :])
        live = page_mass > 0.0
        score = score_rows[k - 1]
        top = jnp.max(jnp.where(live, score, floor_value), axis=1, keepdims=True)
        w = jnp.where(live, page_mass * jnp.exp(score - top), 0.0)
        total = jnp.sum(w, axis=1, keepdims=True)
        w = w.astype(BF16)
        values = [jnp.concatenate([packed_ref[p, 1, 0], packed_ref[p, 1, 1]], axis=1) for p in (a, b)]
        part = jnp.where(jnp.concatenate([first, first], axis=1), dot(w, values[0]), dot(w, values[1]))
        part_send[o, pl.ds(0, 8), :] = jnp.where(head_low, part[:, :128], part[:, 128:])
        stat = jnp.where(lane8 == row8, top, jnp.where(lane8 == row8 + 8, total, 0.0))
        part_send[o, pl.ds(8, 1), :] = jnp.sum(stat, axis=0, keepdims=True)

    def part_copy(k):
        other = at(k)
        return pltpu.make_async_remote_copy(
            src_ref=part_send.at[other, pl.ds(0, 9)],
            dst_ref=part_recv.at[me, pl.ds(0, 9)],
            send_sem=part_sems.at[0],
            recv_sem=part_sems.at[1],
            device_id=(kv_me, other),
            device_id_type=MESH,
        )

    def query_wait(k):
        o = at(k)
        pltpu.make_async_remote_copy(
            src_ref=query_send.at[o],
            dst_ref=query_recv.at[o],
            send_sem=query_send_sem,
            recv_sem=query_recv_sems.at[o],
            device_id=(kv_me, o),
            device_id_type=MESH,
        ).wait_recv()

    def group(i):
        return [GROUP * i + j + 1 for j in range(GROUP)]

    for i in range(seq_count // GROUP):
        others = [k for k in group(i) if k < seq_count]
        for k in others:
            query_wait(k)
        for k in group(i):
            scores(k)
        if i > 0:
            for k in group(i - 1):
                finish(k)
            for k in group(i - 1):
                part_copy(k).start()
    for k in group(i):
        finish(k)
    for k in others:
        part_copy(k).start()
    part_recv[me] = part_send[me]

    def all_of(send, recv, send_sem, recv_sem, n, *rest):
        return pltpu.make_async_remote_copy(
            src_ref=send.at[(pl.ds(0, n), *rest)],
            dst_ref=recv.at[(pl.ds(0, n), *rest)],
            send_sem=send_sem,
            recv_sem=recv_sem,
            device_id=(kv_me, me),
            device_id_type=MESH,
        )

    all_parts = all_of(
        part_send, part_recv, part_sems.at[0], part_sems.at[1], seq_count - 1, pl.ds(0, 9)
    )
    all_parts.wait_recv()
    part_recv_flat = part_recv.reshape(512, 128)
    stats = part_recv_flat[pl.ds(8, 32, stride=16), :]
    top = jnp.concatenate([stats, pltpu.roll(stats, 124, 1)], axis=0)
    total = jnp.concatenate([pltpu.roll(stats, 120, 1), pltpu.roll(stats, 116, 1)], axis=0)
    top = jnp.where(lane < 4, top, 0.0)
    total = jnp.where(lane < 4, total, 0.0)
    best = own
    for r in range(8):
        one = jnp.max(jnp.where(request_col == float(r), top, floor_value), axis=0, keepdims=True)
        best = jnp.where(jnp.logical_and(row8 == r, lane8 < 4), jnp.maximum(best, one), best)
    best_rows = jnp.zeros((64, 128), F32)
    for r in range(8):
        best_rows = jnp.where(request_col == float(r), best[r : r + 1, :], best_rows)
    factor = jnp.exp(top - best_rows)
    scaled = [
        factor[:, h : h + 1]
        * jnp.concatenate(
            [part_recv_flat[pl.ds(k * 4 + h, 32, stride=16), :] for k in range(2)], axis=0
        )
        for h in range(4)
    ]
    gather_b = gather.astype(BF16)
    sums = sum(
        dot(gather_b, piece) for piece in split(jnp.concatenate(scaled + [factor * total], axis=1), 2)
    )
    own_factor = jnp.exp(own - best)
    denominator = sums[:, 512:] + own_factor
    attended = jnp.concatenate(
        [
            (
                sums[:, h * 128 : h * 128 + 128]
                + own_factor[:, h : h + 1] * fresh_flat[pl.ds(16 + (h // 2) * 8, 8), :]
            )
            / denominator[:, h : h + 1]
            for h in range(4)
        ],
        axis=1,
    ).astype(BF16)
    attended_ref[...] = attended

    small[6].wait()

    def sum_block(k):
        other = lax.rem(kv_me + k, kv_count)
        return dot(attended, out_weight[:, pl.ds(pl.multiple_of(other * 512, 512), 512)])

    for k in (2, 1, 3):
        other = lax.rem(kv_me + k, kv_count)
        sum_send[other] = sum_block(k).astype(BF16)
        pltpu.make_async_remote_copy(
            src_ref=sum_send.at[other],
            dst_ref=sum_recv.at[k - 1],
            send_sem=sum_sems.at[0],
            recv_sem=sum_sems.at[1],
            device_id=(other, me),
            device_id_type=MESH,
        ).start()
    mine = sum_block(0)
    all_parts.wait_send()
    all_of(query_send, query_recv, query_send_sem, query_recv_sems.at[0], seq_count - 1).wait_send()
    all_sums = all_of(sum_send, sum_recv, sum_sems.at[0], sum_sems.at[1], kv_count - 1)
    all_sums.wait_recv()
    for k in range(3):
        mine = mine + sum_recv[k].astype(F32)
    projected_ref[...] = mine.astype(BF16)
    all_sums.wait_send()


def early_kernel(
    page_hbm, keep_hbm, weight_hbm, table_hbm, lengths_hbm, out_hbm,
    pages, packed, keep, weight, table, lengths,
    target_rows, count_rows, fold_rows, divisor_rows, page_sem, in_sem, out_sem,
):
    me = lax.axis_index("seq")
    pieces = share()

    def page_copy(i):
        at = pl.ds(i * 8, 8)
        return pltpu.make_async_copy(page_hbm.at[at], pages.at[at], page_sem.at[i])

    def out_copy(i):
        at = pl.ds(i * 8, 8)
        return pltpu.make_async_copy(packed.at[at], out_hbm.at[at], out_sem.at[i])

    @pl.when(pieces > 0)
    def _():
        small = [
            pltpu.make_async_copy(src, dst, in_sem.at[i])
            for i, (src, dst) in enumerate(
                [(table_hbm, table), (lengths_hbm, lengths), (keep_hbm, keep), (weight_hbm, weight)]
            )
        ]
        for copy in small:
            copy.start()
        pl.loop(0, pieces)(lambda i: page_copy(i).start())
        for copy in small:
            copy.wait()
        valid_count, _ = place_pages(table[...], lengths, me)
        rows = (target_rows, count_rows, divisor_rows, fold_rows)
        plan_pages(valid_count, keep, weight, rows)

        @pl.loop(0, pieces)
        def _(i):
            page_copy(i).wait()
            for j in range(8):
                compact_page(i * 8 + j, pages, packed, rows)
            out_copy(i).start()

        pl.loop(0, pieces)(lambda i: out_copy(i).wait())


def write_kernel(packed, mass, attended, projected, early, *rest):
    outs, sems = rest[:4], rest[4]
    pieces = share()

    def packed_copy(i):
        at = pl.ds(i * 8, 8)
        return pltpu.make_async_copy(packed.at[at], outs[0].at[at], sems.at[3 + i])

    small = [
        pltpu.make_async_copy(src, dst, sems.at[i])
        for i, (src, dst) in enumerate(zip((mass, attended, projected), outs[1:]))
    ]
    pl.loop(pieces, 8)(lambda i: packed_copy(i).start())
    for copy in small:
        copy.start()
    for copy in small:
        copy.wait()
    pl.loop(pieces, 8)(lambda i: packed_copy(i).wait())


def per_device(
    page_cache, keep_list, fold_weight, page_table, lengths, queries, fresh_entries, out_weight
):
    anywhere = pl.BlockSpec(memory_space=pl.ANY)
    shapes = [((64, 2, 2, 128, 128), BF16), ((64, 128), BF16), ((8, 512), BF16), ((8, 512), BF16)]
    page_cache, keep_list, fold_weight, table_t, lengths, queries, fresh_entries, out_weight = (
        pltpu.with_memory_space_constraint(x, pltpu.HBM)
        for x in (
            page_cache, keep_list, fold_weight, page_table.T, lengths.reshape(2, 128), queries,
            fresh_entries, out_weight,
        )
    )
    early = pl.pallas_call(
        early_kernel,
        out_shape=pltpu.HBM(*shapes[0]),
        in_specs=[anywhere] * 5,
        out_specs=anywhere,
        scratch_shapes=[
            pltpu.VMEM((64, 2, 2, 128, 128), BF16),
            pltpu.VMEM((64, 2, 2, 128, 128), BF16),
            pltpu.VMEM((64, 128), I32),
            pltpu.VMEM((64, 128), F32),
            pltpu.VMEM((8, 256), I32),
            pltpu.VMEM((2, 128), I32),
            pltpu.VMEM((64, 128), F32),
            pltpu.VMEM((64, 128), F32),
            pltpu.VMEM((3, 64, 128), F32),
            pltpu.VMEM((64, 128), F32),
            pltpu.SemaphoreType.DMA((8,)),
            pltpu.SemaphoreType.DMA((4,)),
            pltpu.SemaphoreType.DMA((8,)),
        ],
        compiler_params=pltpu.CompilerParams(has_side_effects=True, vmem_limit_bytes=36 << 20),
        name="early",
    )(page_cache, keep_list, fold_weight, table_t, lengths)
    results = pl.pallas_call(
        main_kernel,
        out_shape=[pltpu.VMEM(shape, dtype) for shape, dtype in shapes],
        in_specs=[anywhere] * 9,
        out_specs=[pl.BlockSpec(memory_space=pltpu.VMEM)] * 4,
        scratch_shapes=[
            pltpu.VMEM((64, 2, 2, 128, 128), BF16),
            pltpu.VMEM((64, 128), I32),
            pltpu.VMEM((64, 128), F32),
            pltpu.VMEM((8, 256), I32),
            pltpu.VMEM((2, 128), I32),
            pltpu.VMEM((8, 4, 128), BF16),
            pltpu.VMEM((8, 2, 2, 128), BF16),
            pltpu.VMEM((512, 2048), BF16),
            pltpu.VMEM((32, 128), F32),
            pltpu.VMEM((32, 128), F32),
            pltpu.VMEM((32, 8, 128), F32),
            pltpu.VMEM((32, 8, 128), BF16),
            pltpu.VMEM((32, 8, 128), BF16),
            pltpu.VMEM((32, 16, 128), F32),
            pltpu.VMEM((32, 16, 128), F32),
            pltpu.VMEM((4, 8, 512), BF16),
            pltpu.VMEM((4, 8, 512), BF16),
            pltpu.VMEM((64, 128), F32),
            pltpu.VMEM((64, 128), F32),
            pltpu.VMEM((3, 64, 128), F32),
            pltpu.VMEM((64, 128), F32),
            pltpu.VMEM((64, 128), F32),
            pltpu.VMEM((32, 8, 128), F32),
            pltpu.VMEM((1, 128), I32),
            pltpu.SMEM((1, 128), I32),
            pltpu.SemaphoreType.DMA((64 // CHUNK,)),
            pltpu.SemaphoreType.DMA((7,)),
            pltpu.SemaphoreType.DMA,
            pltpu.SemaphoreType.DMA((32,)),
            pltpu.SemaphoreType.DMA((2,)),
            pltpu.SemaphoreType.DMA((2,)),
            pltpu.SemaphoreType.DMA,
        ],
        compiler_params=pltpu.CompilerParams(
            collective_id=0, has_side_effects=True, vmem_limit_bytes=36 << 20
        ),
        name="decode",
    )(
        page_cache, keep_list, fold_weight, table_t, lengths, queries, fresh_entries, out_weight,
        pltpu.with_memory_space_constraint(early, pltpu.HBM),
    )
    return tuple(
        pl.pallas_call(
            write_kernel,
            out_shape=[pltpu.HBM(shape, dtype) for shape, dtype in shapes],
            in_specs=[anywhere] * 5,
            out_specs=[anywhere] * 4,
            scratch_shapes=[pltpu.SemaphoreType.DMA((11,))],
            input_output_aliases={4: 0},
            compiler_params=pltpu.CompilerParams(vmem_limit_bytes=1 << 20),
            name="write",
        )(*results, early)
    )


def solution(mesh):
    placed = (
        P("seq", None, "kv", None, None),
        P("seq", None),
        P("seq", None),
        P(),
        P(),
        P("seq", "kv", None),
        P("seq", None, "kv", None),
        P("kv", None),
    )
    return jax.shard_map(
        per_device,
        mesh=mesh,
        in_specs=placed,
        out_specs=(
            P("seq", None, "kv", None, None),
            P("seq", None),
            P("seq", "kv"),
            P("seq", "kv"),
        ),
        check_vma=False,
    )
```

```python
import functools

import jax
import jax.numpy as jnp
from jax import lax
from jax.experimental import pallas as pl
from jax.experimental.pallas import tpu as pltpu
from jax.sharding import PartitionSpec as P

MESH = pl.DeviceIdType.MESH
F32 = jnp.float32
BF16 = jnp.bfloat16
I32 = jnp.int32
floor_value = -1e30
CHUNK = 16
LEAD = 25
GROUP = 8
PEERS = sorted(
    ((dz, dx, dc) for dz in range(4) for dx in range(4) for dc in range(2)),
    key=lambda d: (-min(d[0], 4 - d[0]) - min(d[1], 4 - d[1]), -d[2], d),
)


def iota(shape, axis):
    return lax.broadcasted_iota(I32, shape, axis)


def split(x, parts):
    out = []
    for _ in range(parts):
        piece = x.astype(BF16)
        out.append(piece)
        x = x - piece.astype(F32)
    return out


def dot(a, b):
    return jnp.dot(a, b, preferred_element_type=F32)


def dot_nt(a, b):
    return lax.dot_general(a, b, (((1,), (1,)), ((), ())), preferred_element_type=F32)


def one_hot_dot(mask, x, parts):
    sel = mask.astype(F32).astype(BF16)
    return sum(dot(sel, piece) for piece in split(x, parts))


def to_row(col, diag):
    return jnp.sum(jnp.where(diag, col, 0.0), axis=0, keepdims=True)


def place_pages(table_t, lengths, me):
    lengths_row = jnp.concatenate([lengths[0:1, :], lengths[1:2, :]], axis=1)
    number = iota((8, 256), 0)
    request = iota((8, 256), 1)
    codes = (jnp.clip(lengths_row - 128 * number, 0, 128) + 256 * (request >> 3)).astype(F32)
    here = iota((64, 256), 0) + 64 * me
    code = jnp.zeros((64, 256), F32)
    for j in range(8):
        code = code + jnp.where(table_t[j : j + 1, :] == here, codes[j : j + 1, :], 0.0)
    code = jnp.sum(code, axis=1, keepdims=True).astype(I32)
    return code & 255, code >> 8


def plan_pages(valid_count, keep, weight, rows):
    target_rows, count_rows, divisor_rows, fold_rows = rows
    lane = iota((64, 128), 1)
    valid = lane < valid_count
    kept = jnp.logical_and(valid, keep[...] > 0)
    dropped = jnp.logical_and(valid, keep[...] == 0)
    kept_flag = kept.astype(F32)
    upper = (iota((128, 128), 0) < iota((128, 128), 1)).astype(F32).astype(BF16)
    position = dot(kept_flag.astype(BF16), upper)
    count = jnp.sum(kept_flag, axis=1, keepdims=True)
    dropped_weight = jnp.where(dropped, weight[...], 0.0)
    weight_sum = jnp.sum(dropped_weight, axis=1, keepdims=True)
    target_rows[...] = jnp.where(kept, position, -1.0)
    count_rows[...] = jnp.broadcast_to(count, (64, 128))
    divisor_rows[...] = jnp.broadcast_to(jnp.maximum(weight_sum, 1.0), (64, 128))
    for i, piece in enumerate(split(dropped_weight, 3)):
        fold_rows[i] = piece.astype(F32)
    lane_f = lane.astype(F32)
    mass = jnp.where(lane_f < count, 1.0, jnp.where(lane_f == count, weight_sum, 0.0)).astype(BF16)
    return mass


def compact_page(p, pages, packed_ref, rows):
    target_rows, count_rows, divisor_rows, fold_rows = rows
    slots = iota((128, 128), 0).astype(F32)
    extra_row = iota((16, 128), 0)
    target = target_rows[pl.ds(p, 1), :]
    picks = jnp.where(slots == target, 1.0, 0.0)
    extra = jnp.where(extra_row == 0, fold_rows[0, pl.ds(p, 1), :], 0.0)
    extra = jnp.where(extra_row == 1, fold_rows[1, pl.ds(p, 1), :], extra)
    extra = jnp.where(extra_row == 2, fold_rows[2, pl.ds(p, 1), :], extra)
    lhs = jnp.concatenate([picks.astype(BF16), extra.astype(BF16)], axis=0)
    page = jnp.concatenate(
        [pages[p, 0, 0], pages[p, 0, 1], pages[p, 1, 0], pages[p, 1, 1]], axis=1
    )
    moved = dot(lhs, page)
    divisor = divisor_rows[pl.ds(p, 1), :]
    folded = jnp.sum(moved[128:136, :], axis=0, keepdims=True)
    at_fold = slots == count_rows[pl.ds(p, 1), :]
    for i in range(4):
        cols = slice(128 * i, 128 * i + 128)
        packed_ref[p, i // 2, i % 2] = jnp.where(
            at_fold, folded[:, cols] / divisor, moved[:128, cols]
        ).astype(BF16)


def share():
    kv_me, me = lax.axis_index("kv"), lax.axis_index("seq")

    def pick(i, values):
        out = values[-1]
        for at in range(len(values) - 1):
            out = jnp.where(i == at, values[at], out)
        return out

    lead = (
        pick(kv_me, (0, 11, 18, 21))
        + pick(me // 8, (0, 13, 27, 29))
        + pick(lax.rem(me // 2, 4), (0, 9, 13, 12))
        + 8 * lax.rem(me, 2)
    )
    return jnp.clip((LEAD - lead + 3) // 4, 0, 8)


def main_kernel(
    page_hbm, keep_hbm, weight_hbm, table_hbm, lengths_hbm, query_hbm, fresh_hbm, out_weight_hbm,
    early,
    packed_ref, mass_ref, attended_ref, projected_ref,
    pages, keep, weight, table, lengths, query, fresh, out_weight,
    query_flat, fresh_flat, query_tiles, query_send, query_recv, part_send, part_recv, sum_send, sum_recv,
    target_rows, count_rows, fold_rows, divisor_rows, mass_rows, score_rows, order_vmem, order,
    page_sem, in_sem, query_send_sem, query_recv_sems, part_sems, sum_sems, order_sem,
):
    kv_count, seq_count = lax.axis_size("kv"), lax.axis_size("seq")
    kv_me, me = lax.axis_index("kv"), lax.axis_index("seq")

    def page_copy(i):
        return pltpu.make_async_copy(
            page_hbm.at[pl.ds(i * CHUNK, CHUNK)], pages.at[pl.ds(i * CHUNK, CHUNK)], page_sem.at[i]
        )

    small = [
        pltpu.make_async_copy(src, dst, in_sem.at[i])
        for i, (src, dst) in enumerate(
            [(table_hbm, table), (query_hbm, query), (lengths_hbm, lengths), (keep_hbm, keep),
             (weight_hbm, weight), (fresh_hbm, fresh), (out_weight_hbm, out_weight)]
        )
    ]
    for copy in small[:5]:
        copy.start()

    @pl.loop(0, 64 // CHUNK)
    def _(i):
        page_copy(i).start()

    where_z, where_x, where_core = me // 8, lax.rem(me // 2, 4), lax.rem(me, 2)

    def at(k):
        dz, dx, dc = PEERS[k - 1]
        return (
            lax.rem(where_z + dz, 4) * 8 + lax.rem(where_x + dx, 4) * 2 + lax.rem(where_core + dc, 2)
        )

    barrier = pltpu.get_barrier_semaphore()
    for k in range(1, seq_count):
        pl.semaphore_signal(barrier, inc=1, device_id=(kv_me, at(k)), device_id_type=MESH)
    for k in range(1, kv_count):
        pl.semaphore_signal(
            barrier, inc=1, device_id=(lax.rem(kv_me + k, kv_count), me), device_id_type=MESH
        )

    small[5].start()
    small[6].start()

    small[0].wait()
    small[1].wait()
    table_t = table[...]
    for r in range(8):
        query_flat[pl.ds(4 * r, 4), :] = query[r].astype(F32)

    lane = iota((64, 128), 1)
    row = iota((64, 128), 0)
    diag = lane == row
    own_pick = (iota((256, 128), 0) == 8 * me + (iota((256, 128), 1) & 7)).astype(F32).astype(BF16)
    keep_lane = (iota((8, 128), 1) >> 3) == iota((8, 128), 0)

    def own_row(x):
        y = dot(x.astype(F32).astype(BF16), own_pick)
        return jnp.sum(jnp.where(keep_lane, y, 0.0), axis=0, keepdims=True)

    inside = iota((1, 128), 1) < 64
    holder_row = jnp.where(inside, own_row(table_t >> 6), -1.0)
    page_row = holder_row * 64.0 + own_row(table_t & 63)

    def to_col(x):
        return jnp.sum(jnp.where(diag, x, 0.0), axis=1, keepdims=True)

    earlier = jnp.logical_and(to_col(holder_row) == holder_row, to_col(page_row) < page_row)
    within_row = jnp.sum(earlier.astype(F32), axis=0, keepdims=True)
    entry_row = jnp.where(inside, 2.0 * holder_row + within_row, -1.0)
    slot_of = (2 * (row & 31) + (row >> 5)).astype(F32)
    entry_pick = (entry_row == slot_of).astype(F32)
    entry_pick_b = entry_pick.astype(BF16)
    picked = dot(
        entry_pick_b,
        jnp.concatenate(
            [jnp.concatenate([query_flat[pl.ds(h, 8, stride=4), :]] * 16, axis=0) for h in range(4)],
            axis=1,
        ).astype(BF16),
    )
    for k in range(2):
        for h in range(4):
            query_tiles.reshape(256, 128)[pl.ds(k * 4 + h, 32, stride=8), :] = picked[
                k * 32 : k * 32 + 32, h * 128 : h * 128 + 128
            ]
    query_send[...] = query_tiles[...].astype(BF16)
    def query_copy(k):
        other = at(k)
        return pltpu.make_async_remote_copy(
            src_ref=query_send.at[other],
            dst_ref=query_recv.at[me],
            send_sem=query_send_sem,
            recv_sem=query_recv_sems.at[me],
            device_id=(kv_me, other),
            device_id_type=MESH,
        )


    request_col = jnp.sum(entry_pick * (lane & 7).astype(F32), axis=1, keepdims=True)
    request_is = ((iota((8, 128), 1) & 7) == iota((8, 128), 0)).astype(F32).astype(BF16)
    gather = dot_nt(request_is, entry_pick_b)

    small[2].wait()
    valid_count, owner = place_pages(table_t, lengths, me)
    owner_col = owner.astype(F32)
    owner_row = jnp.where(inside, to_row(owner_col, diag), -1.0)
    before = jnp.logical_and(owner_col == owner_row, lane < row)
    slot_col = 2.0 * owner_col + jnp.sum(before.astype(F32), axis=1, keepdims=True)
    order_row = jnp.where(slot_col == lane.astype(F32), row.astype(F32), 0.0)
    order_vmem[...] = jnp.sum(order_row, axis=0, keepdims=True).astype(I32)
    order_copy = pltpu.make_async_copy(order_vmem, order, order_sem)
    order_copy.start()

    small[3].wait()
    small[4].wait()
    rows = (target_rows, count_rows, divisor_rows, fold_rows)
    mass = plan_pages(valid_count, keep, weight, rows)
    mass_ref[...] = mass
    mass_rows[...] = mass.astype(F32)

    pl.semaphore_wait(barrier, seq_count - 1 + kv_count - 1)
    for k in range(1, seq_count):
        query_copy(k).start()
    query_recv[me] = query_send[me]

    @pl.loop(0, 64 // CHUNK)
    def _(i):
        page_copy(i).wait()
        for j in range(CHUNK):
            compact_page(i * CHUNK + j, pages, packed_ref, rows)

    small[5].wait()
    for r in range(8):
        for c in range(2):
            both = fresh[r, c].astype(F32)
            for g in range(2):
                fresh_flat[pl.ds((c * 2 + g) * 8 + r, 1), :] = both[g : g + 1, :]
    score_scale = 128 ** -0.5
    lane8 = iota((8, 128), 1)
    row8 = iota((8, 128), 0)
    own = jnp.zeros((8, 128), F32)
    for h in range(4):
        q = query_flat[pl.ds(h, 8, stride=4), :]
        key = fresh_flat[pl.ds((h // 2) * 8, 8), :]
        own = jnp.where(lane8 == h, jnp.sum(q * key, axis=1, keepdims=True) * score_scale, own)

    order_copy.wait()
    first = row8 < 4
    head_low = (row8 & 3) < 2

    def pages_of(o):
        return order[0, 2 * o] & 63, order[0, 2 * o + 1] & 63

    def scores(k):
        o = at(k)
        a, b = pages_of(o)
        q = query_recv[o].astype(F32)
        q = jnp.concatenate(
            [jnp.where(head_low, q, 0.0), jnp.where(head_low, 0.0, q)], axis=1
        ).astype(BF16)
        keys = [jnp.concatenate([packed_ref[p, 0, 0], packed_ref[p, 0, 1]], axis=1) for p in (a, b)]
        score_rows[k - 1] = jnp.where(first, dot_nt(q, keys[0]), dot_nt(q, keys[1])) * score_scale

    def finish(k):
        o = at(k)
        a, b = pages_of(o)
        page_mass = jnp.where(first, mass_rows[pl.ds(a, 1), :], mass_rows[pl.ds(b, 1), :])
        live = page_mass > 0.0
        score = score_rows[k - 1]
        top = jnp.max(jnp.where(live, score, floor_value), axis=1, keepdims=True)
        w = jnp.where(live, page_mass * jnp.exp(score - top), 0.0)
        total = jnp.sum(w, axis=1, keepdims=True)
        w = w.astype(BF16)
        values = [jnp.concatenate([packed_ref[p, 1, 0], packed_ref[p, 1, 1]], axis=1) for p in (a, b)]
        part = jnp.where(jnp.concatenate([first, first], axis=1), dot(w, values[0]), dot(w, values[1]))
        part_send[o, pl.ds(0, 8), :] = jnp.where(head_low, part[:, :128], part[:, 128:])
        stat = jnp.where(lane8 == row8, top, jnp.where(lane8 == row8 + 8, total, 0.0))
        part_send[o, pl.ds(8, 1), :] = jnp.sum(stat, axis=0, keepdims=True)

    def part_copy(k):
        other = at(k)
        return pltpu.make_async_remote_copy(
            src_ref=part_send.at[other, pl.ds(0, 9)],
            dst_ref=part_recv.at[me, pl.ds(0, 9)],
            send_sem=part_sems.at[0],
            recv_sem=part_sems.at[1],
            device_id=(kv_me, other),
            device_id_type=MESH,
        )

    def query_wait(k):
        o = at(k)
        pltpu.make_async_remote_copy(
            src_ref=query_send.at[o],
            dst_ref=query_recv.at[o],
            send_sem=query_send_sem,
            recv_sem=query_recv_sems.at[o],
            device_id=(kv_me, o),
            device_id_type=MESH,
        ).wait_recv()

    def group(i):
        return [GROUP * i + j + 1 for j in range(GROUP)]

    for i in range(seq_count // GROUP):
        others = [k for k in group(i) if k < seq_count]
        for k in others:
            query_wait(k)
        for k in group(i):
            scores(k)
        if i > 0:
            for k in group(i - 1):
                finish(k)
            for k in group(i - 1):
                part_copy(k).start()
    for k in group(i):
        finish(k)
    for k in others:
        part_copy(k).start()
    part_recv[me] = part_send[me]

    def all_of(send, recv, send_sem, recv_sem, n, *rest):
        return pltpu.make_async_remote_copy(
            src_ref=send.at[(pl.ds(0, n), *rest)],
            dst_ref=recv.at[(pl.ds(0, n), *rest)],
            send_sem=send_sem,
            recv_sem=recv_sem,
            device_id=(kv_me, me),
            device_id_type=MESH,
        )

    all_parts = all_of(
        part_send, part_recv, part_sems.at[0], part_sems.at[1], seq_count - 1, pl.ds(0, 9)
    )
    all_parts.wait_recv()
    part_recv_flat = part_recv.reshape(512, 128)
    stats = part_recv_flat[pl.ds(8, 32, stride=16), :]
    top = jnp.concatenate([stats, pltpu.roll(stats, 124, 1)], axis=0)
    total = jnp.concatenate([pltpu.roll(stats, 120, 1), pltpu.roll(stats, 116, 1)], axis=0)
    top = jnp.where(lane < 4, top, 0.0)
    total = jnp.where(lane < 4, total, 0.0)
    best = own
    for r in range(8):
        one = jnp.max(jnp.where(request_col == float(r), top, floor_value), axis=0, keepdims=True)
        best = jnp.where(jnp.logical_and(row8 == r, lane8 < 4), jnp.maximum(best, one), best)
    best_rows = jnp.zeros((64, 128), F32)
    for r in range(8):
        best_rows = jnp.where(request_col == float(r), best[r : r + 1, :], best_rows)
    factor = jnp.exp(top - best_rows)
    scaled = [
        factor[:, h : h + 1]
        * jnp.concatenate(
            [part_recv_flat[pl.ds(k * 4 + h, 32, stride=16), :] for k in range(2)], axis=0
        )
        for h in range(4)
    ]
    gather_b = gather.astype(BF16)
    sums = sum(
        dot(gather_b, piece) for piece in split(jnp.concatenate(scaled + [factor * total], axis=1), 3)
    )
    own_factor = jnp.exp(own - best)
    denominator = sums[:, 512:] + own_factor
    attended = jnp.concatenate(
        [
            (
                sums[:, h * 128 : h * 128 + 128]
                + own_factor[:, h : h + 1] * fresh_flat[pl.ds(16 + (h // 2) * 8, 8), :]
            )
            / denominator[:, h : h + 1]
            for h in range(4)
        ],
        axis=1,
    ).astype(BF16)
    attended_ref[...] = attended

    small[6].wait()

    def sum_block(k):
        other = lax.rem(kv_me + k, kv_count)
        return dot(attended, out_weight[:, pl.ds(pl.multiple_of(other * 512, 512), 512)])

    for k in (2, 1, 3):
        other = lax.rem(kv_me + k, kv_count)
        sum_send[other] = sum_block(k).astype(BF16)
        pltpu.make_async_remote_copy(
            src_ref=sum_send.at[other],
            dst_ref=sum_recv.at[k - 1],
            send_sem=sum_sems.at[0],
            recv_sem=sum_sems.at[1],
            device_id=(other, me),
            device_id_type=MESH,
        ).start()
    mine = sum_block(0)
    all_parts.wait_send()
    all_of(query_send, query_recv, query_send_sem, query_recv_sems.at[0], seq_count - 1).wait_send()
    all_sums = all_of(sum_send, sum_recv, sum_sems.at[0], sum_sems.at[1], kv_count - 1)
    all_sums.wait_recv()
    for k in range(3):
        mine = mine + sum_recv[k].astype(F32)
    projected_ref[...] = mine.astype(BF16)
    all_sums.wait_send()


def early_kernel(
    page_hbm, keep_hbm, weight_hbm, table_hbm, lengths_hbm, out_hbm,
    pages, packed, keep, weight, table, lengths,
    target_rows, count_rows, fold_rows, divisor_rows, page_sem, in_sem, out_sem,
):
    me = lax.axis_index("seq")
    pieces = share()

    def page_copy(i):
        at = pl.ds(i * 8, 8)
        return pltpu.make_async_copy(page_hbm.at[at], pages.at[at], page_sem.at[i])

    def out_copy(i):
        at = pl.ds(i * 8, 8)
        return pltpu.make_async_copy(packed.at[at], out_hbm.at[at], out_sem.at[i])

    @pl.when(pieces > 0)
    def _():
        small = [
            pltpu.make_async_copy(src, dst, in_sem.at[i])
            for i, (src, dst) in enumerate(
                [(table_hbm, table), (lengths_hbm, lengths), (keep_hbm, keep), (weight_hbm, weight)]
            )
        ]
        for copy in small:
            copy.start()
        pl.loop(0, pieces)(lambda i: page_copy(i).start())
        for copy in small:
            copy.wait()
        valid_count, _ = place_pages(table[...], lengths, me)
        rows = (target_rows, count_rows, divisor_rows, fold_rows)
        plan_pages(valid_count, keep, weight, rows)

        @pl.loop(0, pieces)
        def _(i):
            page_copy(i).wait()
            for j in range(8):
                compact_page(i * 8 + j, pages, packed, rows)
            out_copy(i).start()

        pl.loop(0, pieces)(lambda i: out_copy(i).wait())


def write_kernel(packed, mass, attended, projected, early, *rest):
    outs, sems = rest[:4], rest[4]
    pieces = share()

    def packed_copy(i):
        at = pl.ds(i * 8, 8)
        return pltpu.make_async_copy(packed.at[at], outs[0].at[at], sems.at[3 + i])

    small = [
        pltpu.make_async_copy(src, dst, sems.at[i])
        for i, (src, dst) in enumerate(zip((mass, attended, projected), outs[1:]))
    ]
    pl.loop(pieces, 8)(lambda i: packed_copy(i).start())
    for copy in small:
        copy.start()
    for copy in small:
        copy.wait()
    pl.loop(pieces, 8)(lambda i: packed_copy(i).wait())


def per_device(
    page_cache, keep_list, fold_weight, page_table, lengths, queries, fresh_entries, out_weight
):
    anywhere = pl.BlockSpec(memory_space=pl.ANY)
    shapes = [((64, 2, 2, 128, 128), BF16), ((64, 128), BF16), ((8, 512), BF16), ((8, 512), BF16)]
    page_cache, keep_list, fold_weight, table_t, lengths, queries, fresh_entries, out_weight = (
        pltpu.with_memory_space_constraint(x, pltpu.HBM)
        for x in (
            page_cache, keep_list, fold_weight, page_table.T, lengths.reshape(2, 128), queries,
            fresh_entries, out_weight,
        )
    )
    early = pl.pallas_call(
        early_kernel,
        out_shape=pltpu.HBM(*shapes[0]),
        in_specs=[anywhere] * 5,
        out_specs=anywhere,
        scratch_shapes=[
            pltpu.VMEM((64, 2, 2, 128, 128), BF16),
            pltpu.VMEM((64, 2, 2, 128, 128), BF16),
            pltpu.VMEM((64, 128), I32),
            pltpu.VMEM((64, 128), F32),
            pltpu.VMEM((8, 256), I32),
            pltpu.VMEM((2, 128), I32),
            pltpu.VMEM((64, 128), F32),
            pltpu.VMEM((64, 128), F32),
            pltpu.VMEM((3, 64, 128), F32),
            pltpu.VMEM((64, 128), F32),
            pltpu.SemaphoreType.DMA((8,)),
            pltpu.SemaphoreType.DMA((4,)),
            pltpu.SemaphoreType.DMA((8,)),
        ],
        compiler_params=pltpu.CompilerParams(has_side_effects=True, vmem_limit_bytes=36 << 20),
        name="early",
    )(page_cache, keep_list, fold_weight, table_t, lengths)
    results = pl.pallas_call(
        main_kernel,
        out_shape=[pltpu.VMEM(shape, dtype) for shape, dtype in shapes],
        in_specs=[anywhere] * 9,
        out_specs=[pl.BlockSpec(memory_space=pltpu.VMEM)] * 4,
        scratch_shapes=[
            pltpu.VMEM((64, 2, 2, 128, 128), BF16),
            pltpu.VMEM((64, 128), I32),
            pltpu.VMEM((64, 128), F32),
            pltpu.VMEM((8, 256), I32),
            pltpu.VMEM((2, 128), I32),
            pltpu.VMEM((8, 4, 128), BF16),
            pltpu.VMEM((8, 2, 2, 128), BF16),
            pltpu.VMEM((512, 2048), BF16),
            pltpu.VMEM((32, 128), F32),
            pltpu.VMEM((32, 128), F32),
            pltpu.VMEM((32, 8, 128), F32),
            pltpu.VMEM((32, 8, 128), BF16),
            pltpu.VMEM((32, 8, 128), BF16),
            pltpu.VMEM((32, 16, 128), F32),
            pltpu.VMEM((32, 16, 128), F32),
            pltpu.VMEM((4, 8, 512), BF16),
            pltpu.VMEM((4, 8, 512), BF16),
            pltpu.VMEM((64, 128), F32),
            pltpu.VMEM((64, 128), F32),
            pltpu.VMEM((3, 64, 128), F32),
            pltpu.VMEM((64, 128), F32),
            pltpu.VMEM((64, 128), F32),
            pltpu.VMEM((32, 8, 128), F32),
            pltpu.VMEM((1, 128), I32),
            pltpu.SMEM((1, 128), I32),
            pltpu.SemaphoreType.DMA((64 // CHUNK,)),
            pltpu.SemaphoreType.DMA((7,)),
            pltpu.SemaphoreType.DMA,
            pltpu.SemaphoreType.DMA((32,)),
            pltpu.SemaphoreType.DMA((2,)),
            pltpu.SemaphoreType.DMA((2,)),
            pltpu.SemaphoreType.DMA,
        ],
        compiler_params=pltpu.CompilerParams(
            collective_id=0, has_side_effects=True, vmem_limit_bytes=36 << 20
        ),
        name="decode",
    )(
        page_cache, keep_list, fold_weight, table_t, lengths, queries, fresh_entries, out_weight,
        pltpu.with_memory_space_constraint(early, pltpu.HBM),
    )
    return tuple(
        pl.pallas_call(
            write_kernel,
            out_shape=[pltpu.HBM(shape, dtype) for shape, dtype in shapes],
            in_specs=[anywhere] * 5,
            out_specs=[anywhere] * 4,
            scratch_shapes=[pltpu.SemaphoreType.DMA((11,))],
            input_output_aliases={4: 0},
            compiler_params=pltpu.CompilerParams(vmem_limit_bytes=1 << 20),
            name="write",
        )(*results, early)
    )


def solution(mesh):
    placed = (
        P("seq", None, "kv", None, None),
        P("seq", None),
        P("seq", None),
        P(),
        P(),
        P("seq", "kv", None),
        P("seq", None, "kv", None),
        P("kv", None),
    )
    return jax.shard_map(
        per_device,
        mesh=mesh,
        in_specs=placed,
        out_specs=(
            P("seq", None, "kv", None, None),
            P("seq", None),
            P("seq", "kv"),
            P("seq", "kv"),
        ),
        check_vma=False,
    )
```
